32 devices in a mesh: groups: 2 (over y), ctx: 4 (over z), heads: 4 (over x, core).
Axes of the slice: x: 2, y: 2, z: 4, core: 2. Of those that a mesh axis runs over, the one named last changes fastest.
Arguments:
- queries: bfloat16 [2048, 4096], P(('groups', 'ctx'), 'heads'), parts along dimension 0
- keys: bfloat16 [2048, 1024], P(('groups', 'ctx'), 'heads'), parts along dimension 0
- values: bfloat16 [2048, 1024], P(('groups', 'ctx'), 'heads'), parts along dimension 0, may hold values from -6 to 6
- conv_kernel: float32 [32, 6, 11], P('heads')
- head_mix: float32 [8, 4, 4], P('heads')
- norm_gain: float32 [4096], P('heads'), may hold values from 0.5 to 1.5
- bounds: int32 [4], P('groups'), parts along dimension 0, may hold values from 0 to 1024, as said below
Outputs:
- attended: bfloat16 [2048, 4096], P(('groups', 'ctx'), 'heads'), parts along dimension 0
The draws below stay inside these ranges and needn't reach their ends.
There are 2 independent parts, one for each index of `groups`. The reference program is written for one: setup_inputs(seed, part) draws one part's arguments, and reference() takes and returns one part's arrays. A program takes and returns all parts, laid end to end along the dimension named above; an argument that names none is the same for every part. Nothing has to cross between parts.
Inputs may be any that keep to these rules, and one draw needn't show every extreme that they name: bounds[0] < bounds[1], and bounds[1] >= 512.
All inputs are finite; a program needn't handle non-finite values.
Results may differ from the reference program's by a relative error of at most 0.0045.
Values may be sent and summed in bfloat16 or wider, within the bound.
No kernel may reach another device: no remote copies, remote signals or barrier semaphores. Data moves between devices by JAX's collectives and lax.ppermute only.
A program may use at most 64 MiB of HBM per device.

```python
import math
import jax
import jax.numpy as jnp
from jax import lax

QUERY_HEADS = 32
KEY_VALUE_HEADS = 8
HEAD_SIZE = 128
CONV_Q = 6
CONV_K = 11
SEQUENCE_LENGTH = 1024


def grouped_keys(key):
    return jax.random.normal(jax.random.fold_in(key, 11), (SEQUENCE_LENGTH, KEY_VALUE_HEADS * HEAD_SIZE), jnp.float32)


def draw_keys(key, part):
    return grouped_keys(key).astype(jnp.bfloat16)


def draw_queries(key, part):
    drawn_draw = jax.random.normal(jax.random.fold_in(key, 23), (SEQUENCE_LENGTH, QUERY_HEADS * HEAD_SIZE), jnp.float32)
    return drawn_draw.astype(jnp.bfloat16)


def draw_conv_kernel(key, part):
    random_jitter = 0.2 * jax.random.normal(jax.random.fold_in(key, 31), (QUERY_HEADS, CONV_Q, CONV_K), jnp.float32)
    tap_row = jnp.arange(CONV_Q, dtype=jnp.int32)[:, None]
    tap_col = jnp.arange(CONV_K, dtype=jnp.int32)[None, :]
    centre = jnp.where((tap_row == 0) & (tap_col == CONV_K // 2), 1.0, 0.0)
    return random_jitter + centre[None]


def draw_head_mix(key, part):
    heads_per_group = QUERY_HEADS // KEY_VALUE_HEADS
    random_jitter = 0.3 * jax.random.normal(jax.random.fold_in(key, 41), (KEY_VALUE_HEADS, heads_per_group, heads_per_group), jnp.float32)
    return random_jitter + jnp.eye(heads_per_group, dtype=jnp.float32)[None]


def draw_bounds(key, part):
    begin_row = jax.random.randint(jax.random.fold_in(key, 47), (), 0, SEQUENCE_LENGTH // 2 + 1)
    final_len = jax.random.randint(jax.random.fold_in(key, 53), (), SEQUENCE_LENGTH // 2 + 1, SEQUENCE_LENGTH + 1)
    odd_part = part % 2 == 1
    begin_row = jnp.where(odd_part, 0, begin_row)
    final_len = jnp.where(odd_part, final_len, SEQUENCE_LENGTH)
    return jnp.stack([begin_row, final_len]).astype(jnp.int32)


def block_scale(key, dims, split, low, top_value):
    def one(dim, blocks):
        heights = jax.random.uniform(jax.random.fold_in(jax.random.fold_in(key, 6), dim), (blocks,), jnp.float32, low / len(split), top_value / len(split))
        return jnp.repeat(jnp.exp(heights), dims[dim] // blocks).reshape((-1,) + (1,) * (len(dims) - dim - 1))

    factor_of = one(*split[0])
    for cut in split[1:]:
        factor_of = factor_of * one(*cut)
    return factor_of


def gaussian(key, shape, deviation, most, shards=(), kind=jnp.bfloat16):
    array = deviation * jax.random.normal(key, shape, jnp.float32)
    if shards:
        array = array * block_scale(key, shape, shards, -0.22, 0.18)
    return jnp.clip(array, -most, most).astype(kind)


def setup_inputs(seed: int = 0, part: int = 0) -> dict:
    seeds = jax.random.split(jax.random.key(seed), 8)
    own_keys = jax.random.split(jax.random.fold_in(seeds[7], part), 8)
    queries = draw_queries(jax.random.fold_in(jax.random.fold_in(seeds[7], part), 71), part)
    keys = draw_keys(jax.random.fold_in(jax.random.fold_in(seeds[7], part), 71), part)
    values = gaussian(own_keys[2], (SEQUENCE_LENGTH, KEY_VALUE_HEADS * HEAD_SIZE), 1.0, 6.0, ((0, 4), (1, 4)))
    conv_kernel = draw_conv_kernel(jax.random.fold_in(seeds[7], 71), part)
    head_mix = draw_head_mix(jax.random.fold_in(seeds[7], 71), part)
    norm_gain = jnp.clip(1.0 + 0.1 * jax.random.normal(seeds[5], (QUERY_HEADS * HEAD_SIZE,), jnp.float32), 0.5, 1.5)
    bounds = draw_bounds(jax.random.fold_in(jax.random.fold_in(seeds[7], part), 71), part)
    return dict(queries=queries, keys=keys, values=values, conv_kernel=conv_kernel, head_mix=head_mix, norm_gain=norm_gain, bounds=bounds)


NEG_FILL = -1e+30
EPSILON = 1e-06

def reference(queries, keys, values, conv_kernel, head_mix, norm_gain, bounds):
    seq_len = queries.shape[0]
    kv_heads = head_mix.shape[0]
    heads_per_group = head_mix.shape[1]
    head_width = keys.shape[1] // kv_heads
    q_taps = conv_kernel.shape[1]
    k_taps = conv_kernel.shape[2]
    q_edge = q_taps - 1
    k_edge = k_taps // 2
    score_scale = head_width ** (-0.5)
    row_block = math.gcd(seq_len, 512)
    block_count = seq_len // row_block
    start_row = bounds[0]
    end_row = bounds[1]
    query_groups = jnp.transpose(queries.reshape(seq_len, kv_heads, heads_per_group, head_width), (1, 0, 2, 3))
    query_groups = jnp.pad(query_groups, ((0, 0), (q_edge, 0), (0, 0), (0, 0)))
    key_groups = jnp.transpose(keys.reshape(seq_len, kv_heads, head_width), (1, 0, 2))
    key_groups = jnp.pad(key_groups, ((0, 0), (k_edge, k_edge), (0, 0)))
    value_groups = jnp.transpose(values.reshape(seq_len, kv_heads, head_width), (1, 0, 2))
    kernels = conv_kernel.reshape(kv_heads, heads_per_group, q_taps, k_taps)
    gains = norm_gain.reshape(kv_heads, heads_per_group, head_width)
    key_ext_pos = jnp.arange(seq_len + 2 * k_edge, dtype=jnp.int32) - k_edge
    key_pos = jnp.arange(seq_len, dtype=jnp.int32)

    def per_group(operands):
        query_grp, key_grp, value_grp, kernel, mixing, head_gain = operands
        key_wide = key_grp.astype(jnp.float32)
        value_wide = value_grp.astype(jnp.float32)

        def per_block(block_id):
            row_first = block_id * row_block
            query_blk = lax.dynamic_slice_in_dim(query_grp, row_first, row_block + q_edge, 0).astype(jnp.float32)
            raw_scores = jnp.einsum('rmd,kd->mrk', query_blk, key_wide) * score_scale
            row_ext_pos = row_first - q_edge + jnp.arange(row_block + q_edge, dtype=jnp.int32)
            zeroed = jnp.where(key_ext_pos[None, None, :] <= row_ext_pos[None, :, None], raw_scores, 0.0)
            summed = jnp.zeros((heads_per_group, row_block, seq_len), jnp.float32)
            for tap_row in range(q_taps):
                for tap_col in range(k_taps):
                    summed = summed + kernel[:, tap_row, tap_col][:, None, None] * zeroed[:, q_edge - tap_row:q_edge - tap_row + row_block, 2 * k_edge - tap_col:2 * k_edge - tap_col + seq_len]
            row_pos = row_first + jnp.arange(row_block, dtype=jnp.int32)
            row_live = (row_pos >= start_row) & (row_pos < end_row)
            valid_mask = (key_pos[None, :] <= row_pos[:, None]) & row_live[:, None]
            row_max = lax.optimization_barrier(jnp.max(jnp.where(valid_mask[None], summed, NEG_FILL), axis=-1))
            weights = jnp.where(valid_mask[None], jnp.exp(summed - row_max[..., None]), 0.0)
            totals = lax.optimization_barrier(jnp.sum(weights, axis=-1))
            rounded = lax.optimization_barrier(weights.astype(jnp.bfloat16)).astype(jnp.float32)
            accum = jnp.einsum('mrk,kd->mrd', rounded, value_wide)
            probs_out = accum / jnp.where(row_live[None, :], totals, 1.0)[..., None]
            blended = jnp.einsum('ab,brd->ard', mixing, probs_out, precision=lax.Precision.HIGHEST)
            mean_sq = lax.optimization_barrier(jnp.mean(blended * blended, axis=-1, keepdims=True))
            normed = blended * lax.rsqrt(mean_sq + EPSILON) * head_gain[:, None, :]
            return jnp.where(row_live[None, :, None], normed, 0.0).astype(jnp.bfloat16)
        return lax.map(per_block, jnp.arange(block_count, dtype=jnp.int32))
    outputs = lax.map(per_group, (query_groups, key_groups, value_groups, kernels, head_mix, gains))
    outputs = jnp.transpose(outputs, (1, 3, 0, 2, 4))
    return outputs.reshape(seq_len, kv_heads * heads_per_group * head_width)
```

```python
import functools

import jax
import jax.numpy as jnp
from jax import lax
from jax.experimental import pallas as pl
from jax.experimental.pallas import tpu as pltpu
from jax.sharding import PartitionSpec as P

EPSILON = 1e-06
NEG_FILL = -1e30
LANES = 128
HALO = 16
BLOCK = 64
SLOT = 16


def dot_nt(a, b):
    return lax.dot_general(a, b, (((1,), (1,)), ((), ())), preferred_element_type=jnp.float32)


def dot_tn(a, b):
    return lax.dot_general(a, b, (((0,), (0,)), ((), ())), preferred_element_type=jnp.float32)


def fill_key_window(kext, tail, body, head, kv, rows, width):
    for g in range(kv):
        cols = slice(g * width, (g + 1) * width)
        kext[g, :HALO] = tail[:, cols]
        kext[g, HALO : HALO + rows] = body[:, cols]
        if head is None:
            kext[g, HALO + rows :] = jnp.zeros((kext.shape[1] - HALO - rows, width), jnp.bfloat16)
        else:
            kext[g, HALO + rows : 2 * HALO + rows] = head[:, cols]
            rest = kext.shape[1] - 2 * HALO - rows
            kext[g, 2 * HALO + rows :] = jnp.zeros((rest, width), jnp.bfloat16)


def fill_block_keys(rhs, kext, kv, rows, width):
    for g in range(kv):
        for blk in range(rows // BLOCK):
            piece = kext[g, blk * BLOCK : blk * BLOCK + LANES]
            rhs[g, :LANES, blk * width : (blk + 1) * width] = piece
            rhs[g, LANES:, blk * width : (blk + 1) * width] = piece


def folded_keys(kp, taps, rhs, h, g, q_taps, rows, width):
    for a in range(q_taps):
        out = jnp.dot(
            taps[h, a * BLOCK : (a + 1) * BLOCK], rhs[g], preferred_element_type=jnp.float32
        )
        for blk in range(rows // BLOCK):
            piece = out[:, blk * width : (blk + 1) * width]
            high = piece.astype(jnp.bfloat16)
            low = (piece - high.astype(jnp.float32)).astype(jnp.bfloat16)
            at = slice(blk * BLOCK, (blk + 1) * BLOCK)
            kp[at, a * width : (a + 1) * width] = high
            at = slice(rows + blk * BLOCK, rows + (blk + 1) * BLOCK)
            kp[at, a * width : (a + 1) * width] = low


def own_kernel(
    dims,
    q_ref, k_ref, v_ref, e_ref, base_ref, coef_ref,
    qcat_ref, taps_ref, m_ref, l_ref, acc_ref, corner_ref,
    qf, kext, rhs, kp, rolled, zband,
):
    rows, heads, kv, width, q_taps, k_taps = dims
    per = heads // kv
    k_edge = k_taps // 2
    qcols = heads * width
    fill_key_window(kext, e_ref.at[:, qcols:], k_ref, None, kv, rows, width)
    fill_block_keys(rhs, kext, kv, rows, width)
    for h in range(heads):
        for a in range(q_taps):
            row = base_ref[h * q_taps + a : h * q_taps + a + 1, :]
            tile = pltpu.roll(
                jnp.broadcast_to(row, (BLOCK, LANES)), 0, 1, stride=1, stride_axis=0
            )
            high = tile.astype(jnp.bfloat16)
            low = (tile - high.astype(jnp.float32)).astype(jnp.bfloat16)
            taps_ref[h, a * BLOCK : (a + 1) * BLOCK, :LANES] = high
            taps_ref[h, a * BLOCK : (a + 1) * BLOCK, LANES:] = low
    blocks = rows // LANES
    lane = lax.broadcasted_iota(jnp.int32, (rows + HALO, LANES), 1)
    sub = lax.broadcasted_iota(jnp.int32, (rows + HALO, LANES), 0)
    lane_small = lax.broadcasted_iota(jnp.int32, (HALO, LANES), 1)
    packed = jnp.zeros((rows + HALO, LANES), jnp.float32)
    for h in range(heads):
        g = h // per
        cols = slice(h * width, (h + 1) * width)
        qf[:HALO] = e_ref[:, cols].astype(jnp.float32)
        qf[HALO:] = q_ref[:, cols].astype(jnp.float32)
        qcat_ref[h, :, :width] = q_ref[:, cols]
        for a in range(1, q_taps):
            qcat_ref[h, :, a * width : (a + 1) * width] = qf[
                HALO - a : HALO - a + rows
            ].astype(jnp.bfloat16)
        near = jnp.concatenate([q_ref[: LANES - HALO, cols], e_ref[:, cols]], 0)
        pieces = [dot_nt(kext[g, :HALO], near)]
        for blk in range(blocks):
            key_blk = kext[g, HALO + blk * LANES : HALO + (blk + 1) * LANES]
            last = min(rows, (blk + 2) * LANES)
            raw = dot_nt(key_blk, q_ref[blk * LANES : last, cols])
            if last == (blk + 2) * LANES:
                pieces.append(raw[: LANES - HALO, :LANES])
                pieces.append(
                    jnp.where(
                        lane_small < LANES // 2,
                        raw[LANES - HALO :, LANES:],
                        raw[LANES - HALO :, :LANES],
                    )
                )
            else:
                pieces.append(raw)
        ring = jnp.concatenate(pieces, 0)
        for bit in (1, 2, 4):
            ring = jnp.where((sub & bit) != 0, pltpu.roll(ring, LANES - bit, 1), ring)
        moved = []
        for first in range(0, rows + HALO, 8):
            shift = (SLOT * h + HALO - first) % LANES
            part = ring[first : first + 8]
            moved.append(pltpu.roll(part, shift, 1) if shift else part)
        packed = jnp.where((lane // SLOT) == h, jnp.concatenate(moved, 0), packed)
    deltas = range(-k_edge - q_taps + 1, k_edge + 1)
    for order, delta in enumerate(deltas):
        rolled[order, :8] = jnp.zeros((8, LANES), jnp.float32)
        shift = (-delta) % LANES
        rolled[order, 8 : 8 + HALO + rows] = pltpu.roll(packed, shift, 1) if shift else packed
        rolled[order, 8 + HALO + rows :] = jnp.zeros((8, LANES), jnp.float32)
    chunk = 16 * ((rows + HALO) // 16 // 4) if (rows + HALO) % 64 == 0 else 16
    for first in range(0, rows + HALO, chunk):
        total = jnp.zeros((chunk, LANES), jnp.float32)
        for order, delta in enumerate(deltas):
            for a in range(q_taps):
                t = k_edge + a + delta
                if 0 <= t < k_taps:
                    at = 8 + first + k_edge - t
                    row = a * k_taps + t
                    total = total + coef_ref[row : row + 1, :] * rolled[order, at : at + chunk]
        zband[first : first + chunk] = total
    reach = q_taps - 1 + k_edge
    key_id = lax.broadcasted_iota(jnp.int32, (rows, rows), 0)
    row_id = lax.broadcasted_iota(jnp.int32, (rows, rows), 1)
    for h in range(heads):
        g = h // per
        folded_keys(kp, taps_ref, rhs, h, g, q_taps, rows, width)
        both = dot_nt(kp[...], qcat_ref[h])
        scores = both[:rows] + both[rows:]
        shift = (-SLOT * h) % LANES
        corner_ref[h] = pltpu.roll(
            zband[:HALO], (LANES - HALO + shift) % LANES, 1, stride=1, stride_axis=0
        )
        strips = []
        for blk in range(blocks):
            at = HALO + blk * LANES
            tile = pltpu.roll(zband[at : at + LANES], shift, 1, stride=1, stride_axis=0)
            strips.append(jnp.concatenate([tile] * blocks, 1))
        exact = jnp.concatenate(strips, 0)
        scores = jnp.where(row_id - key_id < reach, exact, scores)
        scores = jnp.where(key_id <= row_id, scores, NEG_FILL)
        top = jnp.max(scores, axis=0, keepdims=True)
        weights = jnp.where(key_id <= row_id, jnp.exp(scores - top), 0.0)
        m_ref[h : h + 1, :] = top
        l_ref[h : h + 1, :] = jnp.sum(weights, axis=0, keepdims=True)
        acc_ref[h] = dot_tn(v_ref[:, g * width : (g + 1) * width], weights.astype(jnp.bfloat16))


def step_kernel(
    dims, step,
    qcat_ref, taps_ref, k_ref, head_ref, vt_ref, m_in, l_in, acc_in, corner_ref,
    m_ref, l_ref, acc_ref,
    kext, rhs, kp,
):
    rows, heads, kv, width, q_taps, k_taps = dims
    per = heads // kv
    reach = q_taps - 1 + k_taps // 2

    @pl.when(lax.axis_index("ctx") >= step)
    def _():
        fill_key_window(kext, vt_ref.at[rows:], k_ref, head_ref, kv, rows, width)
        fill_block_keys(rhs, kext, kv, rows, width)
        key_id = lax.broadcasted_iota(jnp.int32, (HALO, LANES), 0)
        row_id = lax.broadcasted_iota(jnp.int32, (HALO, LANES), 1)
        for h in range(heads):
            g = h // per
            folded_keys(kp, taps_ref, rhs, h, g, q_taps, rows, width)
            both = dot_nt(kp[...], qcat_ref[h])
            scores = both[:rows] + both[rows:]
            if step == 1:
                patch = jnp.where(
                    row_id - key_id + HALO < reach, corner_ref[h], scores[rows - HALO :, :LANES]
                )
                last = jnp.concatenate([patch, scores[rows - HALO :, LANES:]], 1)
                scores = jnp.concatenate([scores[: rows - HALO], last], 0)
            old = m_in[h : h + 1, :]
            top = jnp.maximum(old, jnp.max(scores, axis=0, keepdims=True))
            weights = jnp.exp(scores - top)
            decay = jnp.exp(old - top)
            m_ref[h : h + 1, :] = top
            l_ref[h : h + 1, :] = l_in[h : h + 1, :] * decay + jnp.sum(
                weights, axis=0, keepdims=True
            )
            acc_ref[h] = acc_in[h] * decay + dot_tn(
                vt_ref[:rows, g * width : (g + 1) * width], weights.astype(jnp.bfloat16)
            )


def final_kernel(dims, l_ref, acc_ref, mix_ref, gain_ref, bounds_ref, o_ref):
    rows, heads, kv, width, _, _ = dims
    per = heads // kv
    row_pos = lax.axis_index("ctx") * rows + lax.broadcasted_iota(jnp.int32, (rows, 1), 0)
    live = (row_pos >= bounds_ref[0]) & (row_pos < bounds_ref[1])
    for g in range(kv):
        probs = [
            acc_ref[g * per + b] * (1.0 / l_ref[g * per + b : g * per + b + 1, :])
            for b in range(per)
        ]
        for a in range(per):
            blended = mix_ref[g, a, 0] * probs[0]
            for b in range(1, per):
                blended = blended + mix_ref[g, a, b] * probs[b]
            mean_sq = jnp.mean(blended * blended, axis=0, keepdims=True)
            normed = (blended * lax.rsqrt(mean_sq + EPSILON)).T
            h = g * per + a
            normed = normed * gain_ref[:, h * width : (h + 1) * width]
            o_ref[:, h * width : (h + 1) * width] = jnp.where(live, normed, 0.0).astype(jnp.bfloat16)


def in_vmem(count):
    return [pl.BlockSpec(memory_space=pltpu.VMEM)] * count


def per_device(queries, keys, values, conv_kernel, head_mix, norm_gain, bounds):
    rows = queries.shape[0]
    kv, per = head_mix.shape[:2]
    width = keys.shape[1] // kv
    heads, q_taps, k_taps = conv_kernel.shape
    k_edge = k_taps // 2
    count = lax.axis_size("ctx")
    dims = (rows, heads, kv, width, q_taps, k_taps)
    f32, bf16 = jnp.float32, jnp.bfloat16

    def upward(value, first):
        return lax.ppermute(value, "ctx", [(src, src + 1) for src in range(first, count - 1)])

    edges = upward(jnp.concatenate([queries[rows - HALO :], keys[rows - HALO :]], 1), 0)
    key_msg, value_msg = [keys], [values]
    if count > 1:
        key_msg.append(upward(keys, 0))
        tailed = jnp.concatenate([values, edges[:, heads * width :]], 0)
        value_msg.append(upward(tailed, 0))
    for step in range(2, count):
        key_msg.append(upward(key_msg[-1], step - 1))
        value_msg.append(upward(value_msg[-1], step - 1))

    kernel = conv_kernel * width ** (-0.5)
    low = HALO + k_edge - k_taps + 1
    base = jnp.pad(kernel[:, :, ::-1], ((0, 0), (0, 0), (low, LANES - low - k_taps)))
    base = base.reshape(heads * q_taps, LANES)
    offset = jnp.arange(SLOT, dtype=jnp.int32)
    delta = (jnp.arange(k_taps)[None, :] - k_edge - jnp.arange(q_taps)[:, None]).reshape(-1, 1)
    inside = (offset + delta >= 0) & (offset + delta < SLOT) & (offset < q_taps - 1 + k_edge)
    coef = jnp.where(
        inside[:, None, :], kernel.transpose(1, 2, 0).reshape(q_taps * k_taps, heads, 1), 0.0
    ).reshape(q_taps * k_taps, heads * SLOT)
    coef = jnp.pad(coef, ((0, 0), (0, LANES - heads * SLOT)))

    scratch = [
        pltpu.VMEM((kv, rows + LANES, width), bf16),
        pltpu.VMEM((kv, 2 * LANES, rows // BLOCK * width), bf16),
        pltpu.VMEM((2 * rows, q_taps * width), bf16),
    ]
    params = pltpu.CompilerParams(vmem_limit_bytes=28 * 2**20)
    qcat, taps, top, total, acc, corner = pl.pallas_call(
        functools.partial(own_kernel, dims),
        name="own_shard",
        out_shape=(
            pltpu.VMEM((heads, rows, q_taps * width), bf16),
            pltpu.VMEM((heads, q_taps * BLOCK, 2 * LANES), bf16),
            pltpu.VMEM((heads, rows), f32),
            pltpu.VMEM((heads, rows), f32),
            pltpu.VMEM((heads, width, rows), f32),
            pltpu.VMEM((heads, HALO, LANES), f32),
        ),
        in_specs=in_vmem(6),
        out_specs=tuple(in_vmem(6)),
        scratch_shapes=[pltpu.VMEM((rows + HALO, width), f32), *scratch]
        + [
            pltpu.VMEM((q_taps + 2 * k_edge, rows + HALO + 16, LANES), f32),
            pltpu.VMEM((rows + HALO, LANES), f32),
        ],
        compiler_params=params,
        cost_estimate=pl.CostEstimate(flops=6 * 10**9, bytes_accessed=2**20, transcendentals=0),
    )(queries, keys, values, edges, base, coef)
    for step in range(1, count):
        top, total, acc = pl.pallas_call(
            functools.partial(step_kernel, dims, step),
            name="shard_step",
            out_shape=(
                pltpu.VMEM((heads, rows), f32),
                pltpu.VMEM((heads, rows), f32),
                pltpu.VMEM((heads, width, rows), f32),
            ),
            in_specs=in_vmem(9),
            out_specs=tuple(in_vmem(3)),
            scratch_shapes=scratch,
            input_output_aliases={5: 0, 6: 1, 7: 2},
            compiler_params=params,
            cost_estimate=pl.CostEstimate(flops=5 * 10**9, bytes_accessed=2**20, transcendentals=0),
        )(
            qcat, taps, key_msg[step], key_msg[step - 1][:HALO], value_msg[step],
            top, total, acc, corner,
        )
    smem = pl.BlockSpec(memory_space=pltpu.SMEM)
    vmem = pl.BlockSpec(memory_space=pltpu.VMEM)
    return pl.pallas_call(
        functools.partial(final_kernel, dims),
        name="finish",
        out_shape=jax.ShapeDtypeStruct((rows, heads * width), bf16),
        in_specs=[vmem, vmem, smem, vmem, smem],
        out_specs=vmem,
        compiler_params=params,
    )(total, acc, head_mix, norm_gain.reshape(1, -1), bounds)


def solution(mesh):
    return jax.shard_map(
        per_device,
        mesh=mesh,
        in_specs=(
            P(("groups", "ctx"), "heads"),
            P(("groups", "ctx"), "heads"),
            P(("groups", "ctx"), "heads"),
            P("heads", None, None),
            P("heads", None, None),
            P("heads"),
            P("groups"),
        ),
        out_specs=P(("groups", "ctx"), "heads"),
        check_vma=False,
    )
```

```python
import functools

import jax
import jax.numpy as jnp
from jax import lax
from jax.experimental import pallas as pl
from jax.experimental.pallas import tpu as pltpu
from jax.sharding import PartitionSpec as P

EPSILON = 1e-06
NEG_FILL = -1e30
LANES = 128
HALO = 16
BLOCK = 64
SLOT = 16


def dot(a, b):
    return jnp.dot(a, b, preferred_element_type=jnp.float32)


def dot_nt(a, b):
    return lax.dot_general(a, b, (((1,), (1,)), ((), ())), preferred_element_type=jnp.float32)


def dot_tn(a, b, precision=None):
    return lax.dot_general(
        a, b, (((0,), (0,)), ((), ())), precision=precision, preferred_element_type=jnp.float32
    )


def split(value):
    high = value.astype(jnp.bfloat16)
    return high, (value - high.astype(jnp.float32)).astype(jnp.bfloat16)


def fill_windows(rhs, body, after, dims):
    rows, _, kv, width, _, _ = dims
    for g in range(kv):
        cols = slice(g * width, (g + 1) * width)
        for blk in range(rows // BLOCK):
            at = slice(blk * width, (blk + 1) * width)
            first, last = blk * BLOCK, blk * BLOCK + LANES
            if last <= rows:
                piece = body[first:last, cols]
            elif after is None:
                piece = jnp.concatenate(
                    [body[first:rows, cols], jnp.zeros((last - rows, width), jnp.bfloat16)], 0
                )
            else:
                piece = jnp.concatenate([body[first:rows, cols], after[: last - rows, cols]], 0)
            rhs[g, :LANES, at] = piece
            rhs[g, LANES:, at] = piece


def fold_keys(kp, taps, rhs, h, g, dims):
    rows, _, _, width, q_taps, _ = dims
    for a in range(q_taps):
        out = dot(taps[h, a * BLOCK : (a + 1) * BLOCK], rhs[g])
        for blk in range(rows // BLOCK):
            high, low = split(out[:, blk * width : (blk + 1) * width])
            at = blk * BLOCK
            kp[at : at + BLOCK, a * width : (a + 1) * width] = high
            kp[rows + at : rows + at + BLOCK, a * width : (a + 1) * width] = low


def fill_values(vals, body, after, dims):
    rows = dims[0]
    vals[: rows - HALO] = body[HALO:]
    if after is None:
        vals[rows - HALO :] = jnp.zeros((HALO, vals.shape[1]), jnp.bfloat16)
    else:
        vals[rows - HALO :] = after[:HALO]


def pack_kernel(dims, q_hbm, k_hbm, o_ref, sems):
    rows, heads, kv, width, _, _ = dims
    one = pltpu.make_async_copy(
        q_hbm.at[rows - HALO :], o_ref.at[:, : heads * width], sems.at[0]
    )
    two = pltpu.make_async_copy(
        k_hbm.at[rows - HALO :], o_ref.at[:, heads * width :], sems.at[1]
    )
    one.start()
    two.start()
    one.wait()
    two.wait()


def own_kernel(
    dims,
    q_hbm, k_hbm, v_hbm, e_ref, conv_hbm,
    qcat_ref, taps_ref, m_ref, l_ref, acc_ref, corner_ref, kfirst_ref, vfirst_ref,
    q_ref, k_ref, v_ref, conv, coef, qf, rhs, kp0, kp1, sc0, sc1, vals, rolled, zband, sems,
):
    rows, heads, kv, width, q_taps, k_taps = dims
    per = heads // kv
    k_edge = k_taps // 2
    qcols = heads * width
    copies = [
        pltpu.make_async_copy(src, dst, sems.at[i])
        for i, (src, dst) in enumerate(
            ((conv_hbm, conv), (k_hbm, k_ref), (q_hbm, q_ref), (v_hbm, v_ref))
        )
    ]
    for copy in copies:
        copy.start()
    scale = width ** (-0.5)
    copies[0].wait()
    lane8 = lax.broadcasted_iota(jnp.int32, (q_taps, LANES), 1)
    for h in range(heads):
        weights = conv[h] * scale
        base = jnp.zeros((q_taps, LANES), jnp.float32)
        for t in range(k_taps):
            base = jnp.where(lane8 == HALO + k_edge - t, weights[:, t : t + 1], base)
        for a in range(q_taps):
            tile = pltpu.roll(
                jnp.broadcast_to(base[a : a + 1], (BLOCK, LANES)), 0, 1, stride=1, stride_axis=0
            )
            high, low = split(tile)
            taps_ref[h, a * BLOCK : (a + 1) * BLOCK, :LANES] = high
            taps_ref[h, a * BLOCK : (a + 1) * BLOCK, LANES:] = low
    slot = lax.broadcasted_iota(jnp.int32, (heads, LANES), 1)
    spread = jnp.where(
        slot // SLOT == lax.broadcasted_iota(jnp.int32, (heads, LANES), 0), 1.0, 0.0
    ).astype(jnp.float32)
    offset = lax.broadcasted_iota(jnp.int32, (k_taps, LANES), 1) % SLOT
    tap = lax.broadcasted_iota(jnp.int32, (k_taps, LANES), 0)
    reach = q_taps - 1 + k_edge
    for a in range(q_taps):
        lanes = dot_tn(conv[:, a, :] * scale, spread, lax.Precision.HIGHEST)
        source = offset + tap - k_edge - a
        inside = (source >= 0) & (source < SLOT) & (offset < reach)
        coef[a * 16 : a * 16 + k_taps] = jnp.where(inside, lanes, 0.0)
    copies[1].wait()
    fill_windows(rhs, k_ref, None, dims)
    kfirst_ref[...] = k_ref[:BLOCK]
    copies[2].wait()
    blocks = rows // LANES
    lane = lax.broadcasted_iota(jnp.int32, (rows + HALO, LANES), 1)
    sub = lax.broadcasted_iota(jnp.int32, (rows + HALO, LANES), 0)
    lane_small = lax.broadcasted_iota(jnp.int32, (HALO, LANES), 1)
    packed = jnp.zeros((rows + HALO, LANES), jnp.float32)
    for h in range(heads):
        g = h // per
        cols = slice(h * width, (h + 1) * width)
        kcols = slice(g * width, (g + 1) * width)
        qf[:HALO] = e_ref[:, cols].astype(jnp.float32)
        qf[HALO:] = q_ref[:, cols].astype(jnp.float32)
        qcat_ref[h, :, :width] = q_ref[:, cols]
        for a in range(1, q_taps):
            qcat_ref[h, :, a * width : (a + 1) * width] = qf[
                HALO - a : HALO - a + rows
            ].astype(jnp.bfloat16)
        near = jnp.concatenate([q_ref[: LANES - HALO, cols], e_ref[:, cols]], 0)
        pieces = [dot_nt(e_ref[:, qcols + g * width : qcols + (g + 1) * width], near)]
        for blk in range(blocks):
            key_blk = k_ref[blk * LANES : (blk + 1) * LANES, kcols]
            last = min(rows, (blk + 2) * LANES)
            raw = dot_nt(key_blk, q_ref[blk * LANES : last, cols])
            if last == (blk + 2) * LANES:
                pieces.append(raw[: LANES - HALO, :LANES])
                pieces.append(
                    jnp.where(
                        lane_small < LANES // 2,
                        raw[LANES - HALO :, LANES:],
                        raw[LANES - HALO :, :LANES],
                    )
                )
            else:
                pieces.append(raw)
        ring = jnp.concatenate(pieces, 0)
        for bit in (1, 2, 4):
            ring = jnp.where((sub & bit) != 0, pltpu.roll(ring, LANES - bit, 1), ring)
        moved = []
        for first in range(0, rows + HALO, 8):
            shift = (SLOT * h + HALO - first) % LANES
            part = ring[first : first + 8]
            moved.append(pltpu.roll(part, shift, 1) if shift else part)
        packed = jnp.where((lane // SLOT) == h, jnp.concatenate(moved, 0), packed)
    deltas = range(-k_edge - q_taps + 1, k_edge + 1)
    for order, delta in enumerate(deltas):
        rolled[order, :8] = jnp.zeros((8, LANES), jnp.float32)
        shift = (-delta) % LANES
        rolled[order, 8 : 8 + HALO + rows] = pltpu.roll(packed, shift, 1) if shift else packed
        rolled[order, 8 + HALO + rows :] = jnp.zeros((8, LANES), jnp.float32)
    chunk = HALO
    for first in range(0, rows + HALO, chunk):
        total = jnp.zeros((chunk, LANES), jnp.float32)
        for order, delta in enumerate(deltas):
            for a in range(q_taps):
                t = k_edge + a + delta
                if 0 <= t < k_taps:
                    at = 8 + first + k_edge - t
                    row = a * 16 + t
                    total = total + coef[row : row + 1, :] * rolled[order, at : at + chunk]
        zband[first : first + chunk] = total
    zband[rows + HALO :] = jnp.zeros((HALO, LANES), jnp.float32)
    copies[3].wait()
    fill_values(vals, v_ref, None, dims)
    vfirst_ref[...] = v_ref[:HALO]
    key_id = HALO + lax.broadcasted_iota(jnp.int32, (rows, rows), 0)
    row_id = lax.broadcasted_iota(jnp.int32, (rows, rows), 1)
    kps, scs = (kp0, kp1), (sc0, sc1)
    fold_keys(kp0, taps_ref, rhs, 0, 0, dims)
    for h in range(heads):
        g = h // per
        both = dot_nt(kps[h % 2][...], qcat_ref[h])
        scs[h % 2][...] = both[:rows] + both[rows:]
        if h + 1 < heads:
            fold_keys(kps[(h + 1) % 2], taps_ref, rhs, h + 1, (h + 1) // per, dims)
        corner_ref[h] = pltpu.roll(
            zband[: 2 * HALO], (LANES - HALO - SLOT * h) % LANES, 1, stride=1, stride_axis=0
        )
        strips = []
        for blk in range(blocks):
            at = 2 * HALO + blk * LANES
            tile = pltpu.roll(
                zband[at : at + LANES], (HALO - SLOT * h) % LANES, 1, stride=1, stride_axis=0
            )
            strips.append(jnp.concatenate([tile] * blocks, 1))
        exact = jnp.concatenate(strips, 0)
        scores = jnp.where(row_id - key_id < reach, exact, scs[h % 2][...])
        scores = jnp.where(key_id <= row_id, scores, NEG_FILL)
        top = jnp.max(scores, axis=0, keepdims=True)
        weights = jnp.where(key_id <= row_id, jnp.exp(scores - top), 0.0)
        m_ref[h : h + 1, :] = top
        l_ref[h : h + 1, :] = jnp.sum(weights, axis=0, keepdims=True)
        acc_ref[h] = dot_tn(vals[:, g * width : (g + 1) * width], weights.astype(jnp.bfloat16))


def step_kernel(
    dims, step,
    qcat_ref, taps_ref, k_ref, kafter_ref, v_ref, vafter_ref, m_in, l_in, acc_in, corner_ref,
    m_ref, l_ref, acc_ref,
    rhs, kp0, kp1, sc0, sc1, vals,
):
    rows, heads, kv, width, q_taps, k_taps = dims
    per = heads // kv
    reach = q_taps - 1 + k_taps // 2

    @pl.when(lax.axis_index("ctx") >= step)
    def _():
        fill_windows(rhs, k_ref, kafter_ref, dims)
        fill_values(vals, v_ref, vafter_ref, dims)
        key_id = lax.broadcasted_iota(jnp.int32, (2 * HALO, LANES), 0) - HALO
        row_id = lax.broadcasted_iota(jnp.int32, (2 * HALO, LANES), 1)
        kps, scs = (kp0, kp1), (sc0, sc1)
        fold_keys(kp0, taps_ref, rhs, 0, 0, dims)
        for h in range(heads):
            g = h // per
            both = dot_nt(kps[h % 2][...], qcat_ref[h])
            scs[h % 2][...] = both[:rows] + both[rows:]
            if h + 1 < heads:
                fold_keys(kps[(h + 1) % 2], taps_ref, rhs, h + 1, (h + 1) // per, dims)
            if step == 1:
                at = rows - 2 * HALO
                patch = scs[h % 2][at:, :LANES]
                patch = jnp.where(row_id - key_id < reach, corner_ref[h], patch)
                scs[h % 2][at:, :LANES] = jnp.where(key_id <= row_id, patch, NEG_FILL)
            scores = scs[h % 2][...]
            old = m_in[h : h + 1, :]
            top = jnp.maximum(old, jnp.max(scores, axis=0, keepdims=True))
            weights = jnp.exp(scores - top)
            decay = jnp.exp(old - top)
            m_ref[h : h + 1, :] = top
            l_ref[h : h + 1, :] = l_in[h : h + 1, :] * decay + jnp.sum(
                weights, axis=0, keepdims=True
            )
            acc_ref[h] = acc_in[h] * decay + dot_tn(
                vals[:, g * width : (g + 1) * width], weights.astype(jnp.bfloat16)
            )


def final_kernel(dims, count, qcat_ref, taps_ref, m_ref, l_ref, acc_ref, corner_ref,
                 gain_ref, mix_ref, bounds_ref, *rest):
    rows, heads, kv, width, q_taps, k_taps = dims
    per = heads // kv
    reach = q_taps - 1 + k_taps // 2
    key_refs, value_refs = rest[:count], rest[count : 2 * count]
    o_ref, keys, vals = rest[2 * count :]
    place = lax.axis_index("ctx")
    keys[:HALO] = jnp.zeros((HALO, kv * width), jnp.bfloat16)
    keys[3 * HALO :] = jnp.zeros((LANES - 3 * HALO, kv * width), jnp.bfloat16)
    for step in range(count):
        @pl.when(place == step)
        def _(step=step):
            keys[HALO : 3 * HALO] = key_refs[step][: 2 * HALO]
            vals[...] = value_refs[step][:HALO]
    key_id = lax.broadcasted_iota(jnp.int32, (HALO, rows), 0)
    row_id = place * rows + lax.broadcasted_iota(jnp.int32, (HALO, rows), 1)
    row_pos = place * rows + lax.broadcasted_iota(jnp.int32, (rows, 1), 0)
    live = (row_pos >= bounds_ref[0]) & (row_pos < bounds_ref[1])
    for g in range(kv):
        window = keys[:, g * width : (g + 1) * width]
        window = jnp.concatenate([window, window], 0)
        probs = []
        for b in range(per):
            h = g * per + b
            taps = jnp.concatenate(
                [taps_ref[h, a * BLOCK : a * BLOCK + HALO] for a in range(q_taps)], 0
            )
            folded = dot(taps, window)
            folded = jnp.concatenate(
                [folded[a * HALO : (a + 1) * HALO] for a in range(q_taps)], 1
            )
            both = dot_nt(jnp.concatenate(split(folded), 0), qcat_ref[h])
            scores = both[:HALO] + both[HALO:]
            exact = jnp.concatenate([corner_ref[h, HALO:]] * (rows // LANES), 1)
            scores = jnp.where(row_id - key_id < reach, exact, scores)
            scores = jnp.where(key_id <= row_id, scores, NEG_FILL)
            old = m_ref[h : h + 1, :]
            top = jnp.maximum(old, jnp.max(scores, axis=0, keepdims=True))
            weights = jnp.exp(scores - top)
            decay = jnp.exp(old - top)
            total = l_ref[h : h + 1, :] * decay + jnp.sum(weights, axis=0, keepdims=True)
            part = dot_tn(vals[:, g * width : (g + 1) * width], weights.astype(jnp.bfloat16))
            probs.append((acc_ref[h] * decay + part) * (1.0 / total))
        for a in range(per):
            blended = mix_ref[g, a, 0] * probs[0]
            for b in range(1, per):
                blended = blended + mix_ref[g, a, b] * probs[b]
            mean_sq = jnp.mean(blended * blended, axis=0, keepdims=True)
            normed = (blended * lax.rsqrt(mean_sq + EPSILON)).T
            h = g * per + a
            normed = normed * gain_ref[:, h * width : (h + 1) * width]
            o_ref[:, h * width : (h + 1) * width] = jnp.where(live, normed, 0.0).astype(jnp.bfloat16)


VMEM = pl.BlockSpec(memory_space=pltpu.VMEM)
SMEM = pl.BlockSpec(memory_space=pltpu.SMEM)
ANY = pl.BlockSpec(memory_space=pl.ANY)


def cost(flops):
    return pl.CostEstimate(flops=flops, bytes_accessed=2**20, transcendentals=0)


def per_device(queries, keys, values, conv_kernel, head_mix, norm_gain, bounds):
    rows = queries.shape[0]
    kv, per = head_mix.shape[:2]
    width = keys.shape[1] // kv
    heads, q_taps, k_taps = conv_kernel.shape
    count = lax.axis_size("ctx")
    dims = (rows, heads, kv, width, q_taps, k_taps)
    f32, bf16 = jnp.float32, jnp.bfloat16
    params = pltpu.CompilerParams(vmem_limit_bytes=28 * 2**20)

    def upward(value, first):
        return lax.ppermute(value, "ctx", [(src, src + 1) for src in range(first, count - 1)])

    key_msg, value_msg = [keys], [values]
    for step in range(1, count):
        key_msg.append(upward(key_msg[-1], step - 1))
        value_msg.append(upward(value_msg[-1], step - 1))
    edges = upward(
        pl.pallas_call(
            functools.partial(pack_kernel, dims),
            name="pack_edges",
            out_shape=pltpu.VMEM((HALO, (heads + kv) * width), bf16),
            in_specs=[ANY, ANY],
            out_specs=VMEM,
            scratch_shapes=[pltpu.SemaphoreType.DMA((2,))],
            compiler_params=params,
        )(queries, keys),
        0,
    )

    scratch = [
        pltpu.VMEM((kv, 2 * LANES, rows // BLOCK * width), bf16),
        pltpu.VMEM((2 * rows, q_taps * width), bf16),
        pltpu.VMEM((2 * rows, q_taps * width), bf16),
        pltpu.VMEM((rows, rows), f32),
        pltpu.VMEM((rows, rows), f32),
        pltpu.VMEM((rows, kv * width), bf16),
    ]
    state = [
        pltpu.VMEM((heads, rows), f32),
        pltpu.VMEM((heads, rows), f32),
        pltpu.VMEM((heads, width, rows), f32),
    ]
    deltas = q_taps + k_taps - 1
    qcat, taps, top, total, acc, corner, kfirst, vfirst = pl.pallas_call(
        functools.partial(own_kernel, dims),
        name="own_shard",
        out_shape=(
            pltpu.VMEM((heads, rows, q_taps * width), bf16),
            pltpu.VMEM((heads, q_taps * BLOCK, 2 * LANES), bf16),
            *state,
            pltpu.VMEM((heads, 2 * HALO, LANES), f32),
            pltpu.VMEM((BLOCK, kv * width), bf16),
            pltpu.VMEM((HALO, kv * width), bf16),
        ),
        in_specs=[ANY, ANY, ANY, VMEM, ANY],
        out_specs=(VMEM,) * 8,
        scratch_shapes=[
            pltpu.VMEM((rows, heads * width), bf16),
            pltpu.VMEM((rows, kv * width), bf16),
            pltpu.VMEM((rows, kv * width), bf16),
            pltpu.VMEM((heads, q_taps, k_taps), f32),
            pltpu.VMEM((q_taps * 16, LANES), f32),
            pltpu.VMEM((rows + HALO, width), f32),
            *scratch,
            pltpu.VMEM((deltas, rows + HALO + 16, LANES), f32),
            pltpu.VMEM((rows + 2 * HALO, LANES), f32),
            pltpu.SemaphoreType.DMA((4,)),
        ],
        compiler_params=params,
        cost_estimate=cost(6 * 10**9),
    )(queries, keys, values, edges, conv_kernel)
    firsts = [kfirst, *key_msg[1:]], [vfirst, *value_msg[1:]]
    for step in range(1, count):
        top, total, acc = pl.pallas_call(
            functools.partial(step_kernel, dims, step),
            name="shard_step",
            out_shape=tuple(state),
            in_specs=[VMEM] * 10,
            out_specs=(VMEM,) * 3,
            scratch_shapes=scratch,
            input_output_aliases={6: 0, 7: 1, 8: 2},
            compiler_params=params,
            cost_estimate=cost(5 * 10**9),
        )(
            qcat, taps, key_msg[step], firsts[0][step - 1], value_msg[step], firsts[1][step - 1],
            top, total, acc, corner,
        )
    return pl.pallas_call(
        functools.partial(final_kernel, dims, count),
        name="finish",
        out_shape=jax.ShapeDtypeStruct((rows, heads * width), bf16),
        in_specs=[VMEM] * 7 + [SMEM] * 2 + [VMEM] * (2 * count),
        out_specs=VMEM,
        scratch_shapes=[
            pltpu.VMEM((LANES, kv * width), bf16),
            pltpu.VMEM((HALO, kv * width), bf16),
        ],
        compiler_params=params,
    )(
        qcat, taps, top, total, acc, corner, norm_gain.reshape(1, -1), head_mix, bounds,
        *firsts[0], *firsts[1],
    )


def solution(mesh):
    return jax.shard_map(
        per_device,
        mesh=mesh,
        in_specs=(
            P(("groups", "ctx"), "heads"),
            P(("groups", "ctx"), "heads"),
            P(("groups", "ctx"), "heads"),
            P("heads", None, None),
            P("heads", None, None),
            P("heads"),
            P("groups"),
        ),
        out_specs=P(("groups", "ctx"), "heads"),
        check_vma=False,
    )
```

```python
import functools

import jax
import jax.numpy as jnp
from jax import lax
from jax.experimental import pallas as pl
from jax.experimental.pallas import tpu as pltpu
from jax.sharding import PartitionSpec as P

EPSILON = 1e-06
NEG_FILL = -1e30
LANES = 128
HALO = 16
BLOCK = 64
SLOT = 16


def dot(a, b):
    return jnp.dot(a, b, preferred_element_type=jnp.float32)


def dot_nt(a, b):
    return lax.dot_general(a, b, (((1,), (1,)), ((), ())), preferred_element_type=jnp.float32)


def dot_tn(a, b, precision=None):
    return lax.dot_general(
        a, b, (((0,), (0,)), ((), ())), precision=precision, preferred_element_type=jnp.float32
    )


def split(value):
    high = value.astype(jnp.bfloat16)
    return high, (value - high.astype(jnp.float32)).astype(jnp.bfloat16)


def fill_windows(rhs, body, after, dims):
    rows, _, kv, width, _, _ = dims
    for g in range(kv):
        cols = slice(g * width, (g + 1) * width)
        for blk in range(rows // BLOCK):
            at = slice(blk * width, (blk + 1) * width)
            first, last = blk * BLOCK, blk * BLOCK + LANES
            if last <= rows:
                piece = body[first:last, cols]
            elif after is None:
                piece = jnp.concatenate(
                    [body[first:rows, cols], jnp.zeros((last - rows, width), jnp.bfloat16)], 0
                )
            else:
                piece = jnp.concatenate([body[first:rows, cols], after[: last - rows, cols]], 0)
            rhs[g, :LANES, at] = piece
            rhs[g, LANES:, at] = piece


def fold_keys(kp, taps, rhs, h, g, dims):
    rows, _, _, width, q_taps, _ = dims
    for a in range(q_taps):
        out = dot(taps[h, a * BLOCK : (a + 1) * BLOCK], rhs[g])
        for blk in range(rows // BLOCK):
            high, low = split(out[:, blk * width : (blk + 1) * width])
            at = blk * BLOCK
            kp[at : at + BLOCK, a * width : (a + 1) * width] = high
            kp[rows + at : rows + at + BLOCK, a * width : (a + 1) * width] = low


def fill_values(vals, body, after, dims):
    rows = dims[0]
    vals[: rows - HALO] = body[rows + HALO :]
    if after is None:
        vals[rows - HALO : rows] = jnp.zeros((HALO, vals.shape[1]), jnp.bfloat16)
    else:
        vals[rows - HALO : rows] = after[rows : rows + HALO]


def first_window(kv_ref, g, width):
    cols = slice(g * width, (g + 1) * width)
    zeros = jnp.zeros((HALO, width), jnp.bfloat16)
    rest = jnp.zeros((LANES - 3 * HALO, width), jnp.bfloat16)
    window = jnp.concatenate([zeros, kv_ref[: 2 * HALO, cols], rest], 0)
    return jnp.concatenate([window, window], 0)


def first_folded(taps_ref, window, h, q_taps):
    taps = jnp.concatenate(
        [taps_ref[h, a * BLOCK : a * BLOCK + HALO] for a in range(q_taps)], 0
    )
    folded = dot(taps, window)
    folded = jnp.concatenate([folded[a * HALO : (a + 1) * HALO] for a in range(q_taps)], 1)
    return jnp.concatenate(split(folded), 0)


def update(scores, values, at, h, m_in, l_in, acc_in, m_ref, l_ref, acc_ref):
    old = m_in[h : h + 1, :]
    top = jnp.maximum(old, jnp.max(scores, axis=0, keepdims=True))
    weights = jnp.exp(scores - top)
    decay = jnp.exp(old - top)
    m_ref[h : h + 1, :] = top
    l_ref[h : h + 1, :] = l_in[h : h + 1, :] * decay + jnp.sum(weights, axis=0, keepdims=True)
    acc_ref[h] = acc_in[h] * decay + dot_tn(values[:, at], weights.astype(jnp.bfloat16))


def pack_kernel(dims, q_hbm, k_hbm, v_hbm, e_ref, kv_ref, sems):
    rows, heads, _, width, _, _ = dims
    qcols = heads * width
    copies = [
        pltpu.make_async_copy(src, dst, sems.at[i])
        for i, (src, dst) in enumerate(
            (
                (q_hbm.at[rows - HALO :], e_ref.at[:, :qcols]),
                (k_hbm.at[rows - HALO :], e_ref.at[:, qcols:]),
                (k_hbm, kv_ref.at[:rows]),
                (v_hbm, kv_ref.at[rows:]),
            )
        )
    ]
    for copy in copies:
        copy.start()
    for copy in copies:
        copy.wait()


def own_kernel(
    dims,
    q_hbm, kv_ref, e_ref, conv_hbm,
    qcat_ref, taps_ref, m_ref, l_ref, acc_ref, corner_ref,
    q_ref, conv, coef, qf, rhs, kp0, kp1, sc0, sc1, vals, rolled, zband, sems,
):
    rows, heads, kv, width, q_taps, k_taps = dims
    per = heads // kv
    k_edge = k_taps // 2
    qcols = heads * width
    copies = [
        pltpu.make_async_copy(src, dst, sems.at[i])
        for i, (src, dst) in enumerate(
            ((conv_hbm, conv), (q_hbm, q_ref))
        )
    ]
    for copy in copies:
        copy.start()
    scale = width ** (-0.5)
    copies[0].wait()
    lane8 = lax.broadcasted_iota(jnp.int32, (q_taps, LANES), 1)
    for h in range(heads):
        weights = conv[h] * scale
        base = jnp.zeros((q_taps, LANES), jnp.float32)
        for t in range(k_taps):
            base = jnp.where(lane8 == HALO + k_edge - t, weights[:, t : t + 1], base)
        for a in range(q_taps):
            tile = pltpu.roll(
                jnp.broadcast_to(base[a : a + 1], (BLOCK, LANES)), 0, 1, stride=1, stride_axis=0
            )
            high, low = split(tile)
            taps_ref[h, a * BLOCK : (a + 1) * BLOCK, :LANES] = high
            taps_ref[h, a * BLOCK : (a + 1) * BLOCK, LANES:] = low
    slot = lax.broadcasted_iota(jnp.int32, (heads, LANES), 1)
    spread = jnp.where(
        slot // SLOT == lax.broadcasted_iota(jnp.int32, (heads, LANES), 0), 1.0, 0.0
    ).astype(jnp.float32)
    offset = lax.broadcasted_iota(jnp.int32, (k_taps, LANES), 1) % SLOT
    tap = lax.broadcasted_iota(jnp.int32, (k_taps, LANES), 0)
    reach = q_taps - 1 + k_edge
    for a in range(q_taps):
        lanes = dot_tn(conv[:, a, :] * scale, spread, lax.Precision.HIGHEST)
        source = offset + tap - k_edge - a
        inside = (source >= 0) & (source < SLOT) & (offset < reach)
        coef[a * 16 : a * 16 + k_taps] = jnp.where(inside, lanes, 0.0)
    fill_windows(rhs, kv_ref, None, dims)
    copies[1].wait()
    blocks = rows // LANES
    lane = lax.broadcasted_iota(jnp.int32, (rows + HALO, LANES), 1)
    sub = lax.broadcasted_iota(jnp.int32, (rows + HALO, LANES), 0)
    lane_small = lax.broadcasted_iota(jnp.int32, (HALO, LANES), 1)
    packed = jnp.zeros((rows + HALO, LANES), jnp.float32)
    for h in range(heads):
        g = h // per
        cols = slice(h * width, (h + 1) * width)
        kcols = slice(g * width, (g + 1) * width)
        qf[:HALO] = e_ref[:, cols].astype(jnp.float32)
        qf[HALO:] = q_ref[:, cols].astype(jnp.float32)
        qcat_ref[h, :, :width] = q_ref[:, cols]
        for a in range(1, q_taps):
            qcat_ref[h, :, a * width : (a + 1) * width] = qf[
                HALO - a : HALO - a + rows
            ].astype(jnp.bfloat16)
        near = jnp.concatenate([q_ref[: LANES - HALO, cols], e_ref[:, cols]], 0)
        pieces = [dot_nt(e_ref[:, qcols + g * width : qcols + (g + 1) * width], near)]
        for blk in range(blocks):
            key_blk = kv_ref[blk * LANES : (blk + 1) * LANES, kcols]
            last = min(rows, (blk + 2) * LANES)
            raw = dot_nt(key_blk, q_ref[blk * LANES : last, cols])
            if last == (blk + 2) * LANES:
                pieces.append(raw[: LANES - HALO, :LANES])
                pieces.append(
                    jnp.where(
                        lane_small < LANES // 2,
                        raw[LANES - HALO :, LANES:],
                        raw[LANES - HALO :, :LANES],
                    )
                )
            else:
                pieces.append(raw)
        ring = jnp.concatenate(pieces, 0)
        for bit in (1, 2, 4):
            ring = jnp.where((sub & bit) != 0, pltpu.roll(ring, LANES - bit, 1), ring)
        moved = []
        for first in range(0, rows + HALO, 8):
            shift = (SLOT * h + HALO - first) % LANES
            part = ring[first : first + 8]
            moved.append(pltpu.roll(part, shift, 1) if shift else part)
        packed = jnp.where((lane // SLOT) == h, jnp.concatenate(moved, 0), packed)
    deltas = range(-k_edge - q_taps + 1, k_edge + 1)
    for order, delta in enumerate(deltas):
        rolled[order, :8] = jnp.zeros((8, LANES), jnp.float32)
        shift = (-delta) % LANES
        rolled[order, 8 : 8 + HALO + rows] = pltpu.roll(packed, shift, 1) if shift else packed
        rolled[order, 8 + HALO + rows :] = jnp.zeros((8, LANES), jnp.float32)
    chunk = HALO
    for first in range(0, rows + HALO, chunk):
        total = jnp.zeros((chunk, LANES), jnp.float32)
        for order, delta in enumerate(deltas):
            for a in range(q_taps):
                t = k_edge + a + delta
                if 0 <= t < k_taps:
                    at = 8 + first + k_edge - t
                    row = a * 16 + t
                    total = total + coef[row : row + 1, :] * rolled[order, at : at + chunk]
        zband[first : first + chunk] = total
    zband[rows + HALO :] = jnp.zeros((HALO, LANES), jnp.float32)
    fill_values(vals, kv_ref, None, dims)
    key_id = HALO + lax.broadcasted_iota(jnp.int32, (rows, rows), 0)
    row_id = lax.broadcasted_iota(jnp.int32, (rows, rows), 1)
    kps, scs = (kp0, kp1), (sc0, sc1)
    fold_keys(kp0, taps_ref, rhs, 0, 0, dims)
    for h in range(heads):
        g = h // per
        both = dot_nt(kps[h % 2][...], qcat_ref[h])
        scs[h % 2][...] = both[:rows] + both[rows:]
        if h + 1 < heads:
            fold_keys(kps[(h + 1) % 2], taps_ref, rhs, h + 1, (h + 1) // per, dims)
        corner_ref[h] = pltpu.roll(
            zband[: 2 * HALO], (LANES - HALO - SLOT * h) % LANES, 1, stride=1, stride_axis=0
        )
        strips = []
        for blk in range(blocks):
            at = 2 * HALO + blk * LANES
            tile = pltpu.roll(
                zband[at : at + LANES], (HALO - SLOT * h) % LANES, 1, stride=1, stride_axis=0
            )
            strips.append(jnp.concatenate([tile] * blocks, 1))
        exact = jnp.concatenate(strips, 0)
        scores = jnp.where(row_id - key_id < reach, exact, scs[h % 2][...])
        scores = jnp.where(key_id <= row_id, scores, NEG_FILL)
        top = jnp.max(scores, axis=0, keepdims=True)
        weights = jnp.where(key_id <= row_id, jnp.exp(scores - top), 0.0)
        m_ref[h : h + 1, :] = top
        l_ref[h : h + 1, :] = jnp.sum(weights, axis=0, keepdims=True)
        acc_ref[h] = dot_tn(vals[:, g * width : (g + 1) * width], weights.astype(jnp.bfloat16))


def first_positions(dims, place, qcat_ref, taps_ref, kv_ref, corner_ref, state_in, state):
    rows, heads, kv, width, q_taps, k_taps = dims
    per = heads // kv
    reach = q_taps - 1 + k_taps // 2
    key_id = lax.broadcasted_iota(jnp.int32, (HALO, rows), 0)
    row_id = place * rows + lax.broadcasted_iota(jnp.int32, (HALO, rows), 1)
    for g in range(kv):
        window = first_window(kv_ref, g, width)
        at = slice(g * width, (g + 1) * width)
        for h in range(g * per, (g + 1) * per):
            both = dot_nt(first_folded(taps_ref, window, h, q_taps), qcat_ref[h])
            scores = both[:HALO] + both[HALO:]
            exact = jnp.concatenate([corner_ref[h, HALO:]] * (rows // LANES), 1)
            scores = jnp.where(row_id - key_id < reach, exact, scores)
            scores = jnp.where(key_id <= row_id, scores, NEG_FILL)
            update(scores, kv_ref.at[rows : rows + HALO], at, h, *state_in, *state)


def step_kernel(dims, step, count, qcat_ref, taps_ref, corner_ref, m_in, l_in, acc_in, *rest):
    rows, heads, kv, width, q_taps, k_taps = dims
    per = heads // kv
    reach = q_taps - 1 + k_taps // 2
    final = step == count - 1
    messages = rest[: step + 1]
    m_ref, l_ref, acc_ref, rhs, kp0, kp1, sc0, sc1, vals = rest[step + 1 :]
    place = lax.axis_index("ctx")
    body, after = messages[step], messages[step - 1]
    states = (m_in, l_in, acc_in), (m_ref, l_ref, acc_ref)

    @pl.when(place >= step)
    def _():
        fill_windows(rhs, body, after, dims)
        fill_values(vals, body, after, dims)
        if final:
            vals[rows:] = body[rows : rows + HALO]
        key_id = lax.broadcasted_iota(jnp.int32, (2 * HALO, LANES), 0) - HALO
        row_id = lax.broadcasted_iota(jnp.int32, (2 * HALO, LANES), 1)
        kps, scs = (kp0, kp1), (sc0, sc1)

        def fold(h):
            fold_keys(kps[h % 2], taps_ref, rhs, h, h // per, dims)
            if final:
                window = first_window(body, h // per, width)
                kps[h % 2][2 * rows :] = first_folded(taps_ref, window, h, q_taps)

        fold(0)
        for h in range(heads):
            g = h // per
            sc = scs[h % 2]
            both = dot_nt(kps[h % 2][...], qcat_ref[h])
            sc[:rows] = both[:rows] + both[rows : 2 * rows]
            if final:
                sc[rows:] = both[2 * rows : 2 * rows + HALO] + both[2 * rows + HALO :]
            if h + 1 < heads:
                fold(h + 1)
            if step == 1:
                at = slice(rows - 2 * HALO, rows)
                patch = sc[at, :LANES]
                patch = jnp.where(row_id - key_id < reach, corner_ref[h], patch)
                sc[at, :LANES] = jnp.where(key_id <= row_id, patch, NEG_FILL)
            at = slice(g * width, (g + 1) * width)
            update(sc[...], vals, at, h, *states[0], *states[1])

    if final:
        for at in range(step):
            @pl.when(place == at)
            def _(at=at):
                first_positions(
                    dims, place, qcat_ref, taps_ref, messages[at], corner_ref, *states
                )


def final_kernel(dims, l_ref, acc_ref, gain_ref, mix_ref, bounds_ref, o_ref):
    rows, heads, kv, width, _, _ = dims
    per = heads // kv
    row_pos = lax.axis_index("ctx") * rows + lax.broadcasted_iota(jnp.int32, (rows, 1), 0)
    live = (row_pos >= bounds_ref[0]) & (row_pos < bounds_ref[1])
    for g in range(kv):
        probs = [acc_ref[h] * (1.0 / l_ref[h : h + 1, :]) for h in range(g * per, (g + 1) * per)]
        for a in range(per):
            blended = mix_ref[g, a, 0] * probs[0]
            for b in range(1, per):
                blended = blended + mix_ref[g, a, b] * probs[b]
            mean_sq = jnp.mean(blended * blended, axis=0, keepdims=True)
            normed = (blended * lax.rsqrt(mean_sq + EPSILON)).T
            h = g * per + a
            normed = normed * gain_ref[:, h * width : (h + 1) * width]
            o_ref[:, h * width : (h + 1) * width] = jnp.where(live, normed, 0.0).astype(jnp.bfloat16)


VMEM = pl.BlockSpec(memory_space=pltpu.VMEM)
SMEM = pl.BlockSpec(memory_space=pltpu.SMEM)
HBM = pl.BlockSpec(memory_space=pltpu.HBM)


def cost(flops):
    return pl.CostEstimate(flops=flops, bytes_accessed=2**20, transcendentals=0)


def per_device(queries, keys, values, conv_kernel, head_mix, norm_gain, bounds):
    rows = queries.shape[0]
    kv, per = head_mix.shape[:2]
    width = keys.shape[1] // kv
    heads, q_taps, k_taps = conv_kernel.shape
    count = lax.axis_size("ctx")
    dims = (rows, heads, kv, width, q_taps, k_taps)
    f32, bf16 = jnp.float32, jnp.bfloat16
    params = pltpu.CompilerParams(vmem_limit_bytes=28 * 2**20)

    def upward(value, first, hops=1):
        pairs = [(src, src + hops) for src in range(first, count - hops)]
        return lax.ppermute(value, "ctx", pairs)

    columns = kv * width
    queries, keys, values = (
        pltpu.with_memory_space_constraint(value, pltpu.HBM) for value in (queries, keys, values)
    )
    edges, own = pl.pallas_call(
        functools.partial(pack_kernel, dims),
        name="pack",
        out_shape=(
            pltpu.VMEM((HALO, heads * width + columns), bf16),
            pltpu.VMEM((2 * rows, columns), bf16),
        ),
        in_specs=[HBM, HBM, HBM],
        out_specs=(VMEM, VMEM),
        scratch_shapes=[pltpu.SemaphoreType.DMA((4,))],
        compiler_params=params,
    )(queries, keys, values)
    edges = upward(edges, 0)
    messages = [own, upward(own, 0)]
    for step in range(2, count):
        messages.append(upward(own, 0, 2) if step == 2 else upward(messages[-1], step - 1))

    def scratch(extra):
        return [
            pltpu.VMEM((kv, 2 * LANES, rows // BLOCK * width), bf16),
            pltpu.VMEM((2 * (rows + extra), q_taps * width), bf16),
            pltpu.VMEM((2 * (rows + extra), q_taps * width), bf16),
            pltpu.VMEM((rows + extra, rows), f32),
            pltpu.VMEM((rows + extra, rows), f32),
            pltpu.VMEM((rows + extra, columns), bf16),
        ]

    state = [
        pltpu.VMEM((heads, rows), f32),
        pltpu.VMEM((heads, rows), f32),
        pltpu.VMEM((heads, width, rows), f32),
    ]
    deltas = q_taps + k_taps - 1
    qcat, taps, top, total, acc, corner = pl.pallas_call(
        functools.partial(own_kernel, dims),
        name="own_shard",
        out_shape=(
            pltpu.VMEM((heads, rows, q_taps * width), bf16),
            pltpu.VMEM((heads, q_taps * BLOCK, 2 * LANES), bf16),
            *state,
            pltpu.VMEM((heads, 2 * HALO, LANES), f32),
        ),
        in_specs=[HBM, VMEM, VMEM, HBM],
        out_specs=(VMEM,) * 6,
        scratch_shapes=[
            pltpu.VMEM((rows, heads * width), bf16),
            pltpu.VMEM((heads, q_taps, k_taps), f32),
            pltpu.VMEM((q_taps * 16, LANES), f32),
            pltpu.VMEM((rows + HALO, width), f32),
            *scratch(0),
            pltpu.VMEM((deltas, rows + HALO + 16, LANES), f32),
            pltpu.VMEM((rows + 2 * HALO, LANES), f32),
            pltpu.SemaphoreType.DMA((2,)),
        ],
        compiler_params=params,
        cost_estimate=cost(6 * 10**9),
    )(queries, own, edges, conv_kernel)
    for step in range(1, count):
        top, total, acc = pl.pallas_call(
            functools.partial(step_kernel, dims, step, count),
            name="shard_step",
            out_shape=tuple(state),
            in_specs=[VMEM] * (7 + step),
            out_specs=(VMEM,) * 3,
            scratch_shapes=scratch(HALO if step == count - 1 else 0),
            input_output_aliases={3: 0, 4: 1, 5: 2},
            compiler_params=params,
            cost_estimate=cost(5 * 10**9),
        )(qcat, taps, corner, top, total, acc, *messages[: step + 1])
    return pl.pallas_call(
        functools.partial(final_kernel, dims),
        name="finish",
        out_shape=jax.ShapeDtypeStruct((rows, heads * width), bf16),
        in_specs=[VMEM] * 3 + [SMEM] * 2,
        out_specs=VMEM,
        compiler_params=params,
    )(total, acc, norm_gain.reshape(1, -1), head_mix, bounds)


def solution(mesh):
    return jax.shard_map(
        per_device,
        mesh=mesh,
        in_specs=(
            P(("groups", "ctx"), "heads"),
            P(("groups", "ctx"), "heads"),
            P(("groups", "ctx"), "heads"),
            P("heads", None, None),
            P("heads", None, None),
            P("heads"),
            P("groups"),
        ),
        out_specs=P(("groups", "ctx"), "heads"),
        check_vma=False,
    )
```

```python
import functools

import jax
import jax.numpy as jnp
from jax import lax
from jax.experimental import pallas as pl
from jax.experimental.pallas import tpu as pltpu
from jax.sharding import PartitionSpec as P

EPSILON = 1e-06
NEG_FILL = -1e30
LANES = 128
HALO = 16
BLOCK = 64
SLOT = 16


def dot(a, b):
    return jnp.dot(a, b, preferred_element_type=jnp.float32)


def dot_nt(a, b):
    return lax.dot_general(a, b, (((1,), (1,)), ((), ())), preferred_element_type=jnp.float32)


def dot_tn(a, b, precision=None):
    return lax.dot_general(
        a, b, (((0,), (0,)), ((), ())), precision=precision, preferred_element_type=jnp.float32
    )


def split(value):
    high = value.astype(jnp.bfloat16)
    return high, (value - high.astype(jnp.float32)).astype(jnp.bfloat16)


def slot_lane(h):
    return 2 * SLOT * (h % 4) + SLOT * (h // 4)


def fill_windows(rhs, body, after, dims):
    rows, _, kv, width, _, _ = dims
    for g in range(kv):
        cols = slice(g * width, (g + 1) * width)
        for blk in range(rows // BLOCK):
            at = slice(blk * width, (blk + 1) * width)
            first, last = blk * BLOCK, blk * BLOCK + LANES
            if last <= rows:
                piece = body[first:last, cols]
            elif after is None:
                piece = jnp.concatenate(
                    [body[first:rows, cols], jnp.zeros((last - rows, width), jnp.bfloat16)], 0
                )
            else:
                piece = jnp.concatenate([body[first:rows, cols], after[: last - rows, cols]], 0)
            rhs[g, :LANES, at] = piece
            rhs[g, LANES:, at] = piece


def fold_keys(kp, taps, rhs, h, g, dims):
    rows, _, _, width, q_taps, _ = dims
    for a in range(q_taps):
        out = dot(taps[h, a * BLOCK : (a + 1) * BLOCK], rhs[g])
        for blk in range(rows // BLOCK):
            high, low = split(out[:, blk * width : (blk + 1) * width])
            at = blk * BLOCK
            kp[at : at + BLOCK, a * width : (a + 1) * width] = high
            kp[rows + at : rows + at + BLOCK, a * width : (a + 1) * width] = low


def fill_values(vals, body, after, dims):
    rows = dims[0]
    vals[: rows - HALO] = body[rows + HALO :]
    if after is None:
        vals[rows - HALO : rows] = jnp.zeros((HALO, vals.shape[1]), jnp.bfloat16)
    else:
        vals[rows - HALO : rows] = after[rows : rows + HALO]


def first_window(kv_ref, g, width):
    cols = slice(g * width, (g + 1) * width)
    zeros = jnp.zeros((HALO, width), jnp.bfloat16)
    rest = jnp.zeros((LANES - 3 * HALO, width), jnp.bfloat16)
    window = jnp.concatenate([zeros, kv_ref[: 2 * HALO, cols], rest], 0)
    return jnp.concatenate([window, window], 0)


def first_folded(taps_ref, window, h, q_taps):
    taps = jnp.concatenate(
        [taps_ref[h, a * BLOCK : a * BLOCK + HALO] for a in range(q_taps)], 0
    )
    folded = dot(taps, window)
    folded = jnp.concatenate([folded[a * HALO : (a + 1) * HALO] for a in range(q_taps)], 1)
    return jnp.concatenate(split(folded), 0)


def update(scores, values, at, h, m_in, l_in, acc_in, m_ref, l_ref, acc_ref):
    old = m_in[h : h + 1, :]
    top = jnp.maximum(old, jnp.max(scores, axis=0, keepdims=True))
    weights = jnp.exp(scores - top)
    decay = jnp.exp(old - top)
    m_ref[h : h + 1, :] = top
    l_ref[h : h + 1, :] = l_in[h : h + 1, :] * decay + jnp.sum(weights, axis=0, keepdims=True)
    acc_ref[h] = acc_in[h] * decay + dot_tn(values[:, at], weights.astype(jnp.bfloat16))


def pack_kernel(dims, q_hbm, k_hbm, v_hbm, e_ref, kv_ref, sems):
    rows, heads, _, width, _, _ = dims
    qcols = heads * width
    copies = [
        pltpu.make_async_copy(src, dst, sems.at[i])
        for i, (src, dst) in enumerate(
            (
                (q_hbm.at[rows - HALO :], e_ref.at[:, :qcols]),
                (k_hbm.at[rows - HALO :], e_ref.at[:, qcols:]),
                (k_hbm, kv_ref.at[:rows]),
                (v_hbm, kv_ref.at[rows:]),
            )
        )
    ]
    for copy in copies:
        copy.start()
    for copy in copies:
        copy.wait()


def own_kernel(
    dims,
    q_hbm, kv_ref, e_ref, conv_hbm,
    qcat_ref, taps_ref, m_ref, l_ref, acc_ref, corner_ref,
    q_ref, conv, coef, qf, rhs, kp0, kp1, sc, vals, rolled, zband, packed_ref, sems,
):
    rows, heads, kv, width, q_taps, k_taps = dims
    per = heads // kv
    k_edge = k_taps // 2
    qcols = heads * width
    copies = [
        pltpu.make_async_copy(src, dst, sems.at[i])
        for i, (src, dst) in enumerate(
            ((conv_hbm, conv), (q_hbm, q_ref))
        )
    ]
    for copy in copies:
        copy.start()
    scale = width ** (-0.5)
    copies[0].wait()
    fill_windows(rhs, kv_ref, None, dims)
    fill_values(vals, kv_ref, None, dims)
    lane8 = lax.broadcasted_iota(jnp.int32, (heads, LANES), 1)
    bases = []
    owner = lane8 // (2 * SLOT) + 4 * ((lane8 // SLOT) % 2)
    spread = jnp.where(
        owner == lax.broadcasted_iota(jnp.int32, (heads, LANES), 0), 1.0, 0.0
    ).astype(jnp.float32)
    offset = lax.broadcasted_iota(jnp.int32, (k_taps, LANES), 1) % SLOT
    tap = lax.broadcasted_iota(jnp.int32, (k_taps, LANES), 0)
    reach = q_taps - 1 + k_edge
    for a in range(q_taps):
        weights = conv[a] * scale
        base = jnp.zeros((heads, LANES), jnp.float32)
        for t in range(k_taps):
            base = jnp.where(lane8 == HALO + k_edge - t, weights[:, t : t + 1], base)
        bases.append(base)
        lanes = dot_tn(weights, spread, lax.Precision.HIGHEST)
        source = offset + tap - k_edge - a
        inside = (source >= 0) & (source < SLOT) & (offset < reach)
        coef[a * 16 : a * 16 + k_taps] = jnp.where(inside, lanes, 0.0)
    copies[1].wait()
    blocks = rows // LANES
    tall = rows + HALO
    lane = lax.broadcasted_iota(jnp.int32, (tall, LANES), 1)
    sub = lax.broadcasted_iota(jnp.int32, (tall, LANES), 0)
    lane_small = lax.broadcasted_iota(jnp.int32, (HALO, LANES), 1)
    packs = [jnp.zeros((tall, LANES), jnp.float32) for _ in range(2)]
    for h in range(heads):
        g = h // per
        cols = slice(h * width, (h + 1) * width)
        kcols = slice(g * width, (g + 1) * width)
        for a in range(q_taps):
            tile = pltpu.roll(
                jnp.broadcast_to(bases[a][h : h + 1], (BLOCK, LANES)),
                0, 1, stride=1, stride_axis=0,
            )
            high, low = split(tile)
            taps_ref[h, a * BLOCK : (a + 1) * BLOCK, :LANES] = high
            taps_ref[h, a * BLOCK : (a + 1) * BLOCK, LANES:] = low
        qf[:HALO] = e_ref[:, cols].astype(jnp.float32)
        qf[HALO:] = q_ref[:, cols].astype(jnp.float32)
        qcat_ref[h, :, :width] = q_ref[:, cols]
        for a in range(1, q_taps):
            qcat_ref[h, :, a * width : (a + 1) * width] = qf[
                HALO - a : HALO - a + rows
            ].astype(jnp.bfloat16)
        near = jnp.concatenate([q_ref[: LANES - HALO, cols], e_ref[:, cols]], 0)
        pieces = [dot_nt(e_ref[:, qcols + g * width : qcols + (g + 1) * width], near)]
        for blk in range(blocks):
            key_blk = kv_ref[blk * LANES : (blk + 1) * LANES, kcols]
            last = min(rows, (blk + 2) * LANES)
            raw = dot_nt(key_blk, q_ref[blk * LANES : last, cols])
            if last == (blk + 2) * LANES:
                pieces.append(raw[: LANES - HALO, :LANES])
                pieces.append(
                    jnp.where(
                        lane_small < LANES // 2,
                        raw[LANES - HALO :, LANES:],
                        raw[LANES - HALO :, :LANES],
                    )
                )
            else:
                pieces.append(raw)
        ring = jnp.concatenate(pieces, 0)
        moved = []
        for first in range(0, tall, 8):
            shift = (slot_lane(h) + HALO - first) % LANES
            part = ring[first : first + 8]
            moved.append(pltpu.roll(part, shift, 1) if shift else part)
        mine = (lane - slot_lane(h)) % LANES < 2 * SLOT
        packs[h // 4] = jnp.where(mine, jnp.concatenate(moved, 0), packs[h // 4])
    for i in range(2 if heads > 4 else 1):
        for bit in (1, 2, 4):
            packs[i] = jnp.where(
                (sub & bit) != 0, pltpu.roll(packs[i], LANES - bit, 1), packs[i]
            )
    packed_ref[...] = jnp.where((lane // SLOT) % 2 == 0, packs[0], packs[1])
    deltas = list(enumerate(range(-k_edge - q_taps + 1, k_edge + 1)))

    def roll_unit(order, delta):
        rolled[order, :8] = jnp.zeros((8, LANES), jnp.float32)
        shift = (-delta) % LANES
        value = packed_ref[...]
        rolled[order, 8 : 8 + tall] = pltpu.roll(value, shift, 1) if shift else value
        rolled[order, 8 + tall :] = jnp.zeros((8, LANES), jnp.float32)

    def band_unit(first):
        total = jnp.zeros((HALO, LANES), jnp.float32)
        for order, delta in deltas:
            for a in range(q_taps):
                t = k_edge + a + delta
                if 0 <= t < k_taps:
                    at = 8 + first + k_edge - t
                    row = a * 16 + t
                    total = total + coef[row : row + 1, :] * rolled[order, at : at + HALO]
        zband[first : first + HALO] = total

    units = [functools.partial(roll_unit, *pair) for pair in deltas]
    units += [functools.partial(band_unit, first) for first in range(0, tall, HALO)]
    zband[tall:] = jnp.zeros((HALO, LANES), jnp.float32)
    key_id = HALO + lax.broadcasted_iota(jnp.int32, (rows, rows), 0)
    row_id = lax.broadcasted_iota(jnp.int32, (rows, rows), 1)

    def finish_head(h):
        g = h // per
        base = slot_lane(h)
        corner_ref[h] = pltpu.roll(
            zband[: 2 * HALO], (LANES - HALO - base) % LANES, 1, stride=1, stride_axis=0
        )
        strips = []
        for blk in range(blocks):
            at = 2 * HALO + blk * LANES
            tile = pltpu.roll(
                zband[at : at + LANES], (HALO - base) % LANES, 1, stride=1, stride_axis=0
            )
            strips.append(jnp.concatenate([tile] * blocks, 1))
        exact = jnp.concatenate(strips, 0)
        scores = jnp.where(row_id - key_id < reach, exact, sc[h])
        scores = jnp.where(key_id <= row_id, scores, NEG_FILL)
        top = jnp.max(scores, axis=0, keepdims=True)
        weights = jnp.where(key_id <= row_id, jnp.exp(scores - top), 0.0)
        m_ref[h : h + 1, :] = top
        l_ref[h : h + 1, :] = jnp.sum(weights, axis=0, keepdims=True)
        acc_ref[h] = dot_tn(vals[:, g * width : (g + 1) * width], weights.astype(jnp.bfloat16))

    kps = (kp0, kp1)
    early = max(1, heads - 3)
    share = -(-len(units) // early)
    done = 0
    for h in range(heads):
        fold_keys(kps[h % 2], taps_ref, rhs, h, h // per, dims)
        if h < early:
            for unit in units[h * share : (h + 1) * share]:
                unit()
        else:
            for _ in range(2):
                if done < h:
                    finish_head(done)
                    done += 1
        both = dot_nt(kps[h % 2][...], qcat_ref[h])
        sc[h] = both[:rows] + both[rows:]
    for h in range(done, heads):
        finish_head(h)


def first_positions(dims, place, qcat_ref, taps_ref, kv_ref, corner_ref, state_in, state):
    rows, heads, kv, width, q_taps, k_taps = dims
    per = heads // kv
    reach = q_taps - 1 + k_taps // 2
    key_id = lax.broadcasted_iota(jnp.int32, (HALO, rows), 0)
    row_id = place * rows + lax.broadcasted_iota(jnp.int32, (HALO, rows), 1)
    for g in range(kv):
        window = first_window(kv_ref, g, width)
        at = slice(g * width, (g + 1) * width)
        for h in range(g * per, (g + 1) * per):
            both = dot_nt(first_folded(taps_ref, window, h, q_taps), qcat_ref[h])
            scores = both[:HALO] + both[HALO:]
            exact = jnp.concatenate([corner_ref[h, HALO:]] * (rows // LANES), 1)
            scores = jnp.where(row_id - key_id < reach, exact, scores)
            scores = jnp.where(key_id <= row_id, scores, NEG_FILL)
            update(scores, kv_ref.at[rows : rows + HALO], at, h, *state_in, *state)


def needed(routes, step, count):
    reads = {routes[at][step - i] for at in range(step, count) for i in range(2)}
    if step == count - 1:
        reads |= {routes[at][at] for at in range(step)}
    return sorted(reads)


def step_kernel(dims, step, count, routes, qcat_ref, taps_ref, corner_ref, m_in, l_in, acc_in, *rest):
    rows, heads, kv, width, q_taps, k_taps = dims
    per = heads // kv
    reach = q_taps - 1 + k_taps // 2
    final = step == count - 1
    messages = dict(zip(needed(routes, step, count), rest[:-9]))
    m_ref, l_ref, acc_ref, rhs, kp0, kp1, sc0, sc1, vals = rest[-9:]
    place = lax.axis_index("ctx")
    states = (m_in, l_in, acc_in), (m_ref, l_ref, acc_ref)

    @pl.when(place >= step)
    def _():
        pairs = [(routes[at][step], routes[at][step - 1]) for at in range(step, count)]
        for pair in sorted(set(pairs)):
            here = [step + i for i, other in enumerate(pairs) if other == pair]

            def load(body=messages[pair[0]], after=messages[pair[1]]):
                fill_windows(rhs, body, after, dims)
                fill_values(vals, body, after, dims)

            if len(here) == len(pairs):
                load()
            else:
                pl.when(functools.reduce(jnp.logical_or, [place == at for at in here]))(load)
        body = messages[routes[count - 1][step]]
        if final:
            vals[rows:] = body[rows : rows + HALO]
        key_id = lax.broadcasted_iota(jnp.int32, (2 * HALO, LANES), 0) - HALO
        row_id = lax.broadcasted_iota(jnp.int32, (2 * HALO, LANES), 1)
        kps, scs = (kp0, kp1), (sc0, sc1)

        def fold(h):
            fold_keys(kps[h % 2], taps_ref, rhs, h, h // per, dims)
            if final:
                window = first_window(body, h // per, width)
                kps[h % 2][2 * rows :] = first_folded(taps_ref, window, h, q_taps)

        fold(0)
        for h in range(heads):
            g = h // per
            sc = scs[h % 2]
            both = dot_nt(kps[h % 2][...], qcat_ref[h])
            sc[:rows] = both[:rows] + both[rows : 2 * rows]
            if final:
                sc[rows:] = both[2 * rows : 2 * rows + HALO] + both[2 * rows + HALO :]
            if h + 1 < heads:
                fold(h + 1)
            if step == 1:
                at = slice(rows - 2 * HALO, rows)
                patch = sc[at, :LANES]
                patch = jnp.where(row_id - key_id < reach, corner_ref[h], patch)
                sc[at, :LANES] = jnp.where(key_id <= row_id, patch, NEG_FILL)
            at = slice(g * width, (g + 1) * width)
            update(sc[...], vals, at, h, *states[0], *states[1])

    if final:
        for at in range(step):
            @pl.when(place == at)
            def _(at=at):
                first_positions(
                    dims, place, qcat_ref, taps_ref, messages[routes[at][at]], corner_ref, *states
                )


def final_kernel(dims, l_ref, acc_ref, gain_ref, mix_ref, bounds_ref, o_ref):
    rows, heads, kv, width, _, _ = dims
    per = heads // kv
    row_pos = lax.axis_index("ctx") * rows + lax.broadcasted_iota(jnp.int32, (rows, 1), 0)
    live = (row_pos >= bounds_ref[0]) & (row_pos < bounds_ref[1])
    for g in range(kv):
        probs = [acc_ref[h] * (1.0 / l_ref[h : h + 1, :]) for h in range(g * per, (g + 1) * per)]
        for a in range(per):
            blended = mix_ref[g, a, 0] * probs[0]
            for b in range(1, per):
                blended = blended + mix_ref[g, a, b] * probs[b]
            mean_sq = jnp.mean(blended * blended, axis=0, keepdims=True)
            normed = (blended * lax.rsqrt(mean_sq + EPSILON)).T
            h = g * per + a
            normed = normed * gain_ref[:, h * width : (h + 1) * width]
            o_ref[:, h * width : (h + 1) * width] = jnp.where(live, normed, 0.0).astype(jnp.bfloat16)


VMEM = pl.BlockSpec(memory_space=pltpu.VMEM)
SMEM = pl.BlockSpec(memory_space=pltpu.SMEM)
HBM = pl.BlockSpec(memory_space=pltpu.HBM)


def send(value, pairs):
    return lax.ppermute(value, "ctx", pairs)


def spread_messages(own, count):
    if count == 4:
        ahead = send(own, [(0, 2), (2, 3)])
        near = send(own, [(0, 1), (1, 2)])
        skip = send(own, [(1, 3)])
        return [own, ahead, skip, near], [[0], [0, 3], [0, 3, 1], [0, 1, 2, 4]]
    first = send(own, [(at, at + 1) for at in range(count - 1)])
    return [own, first], [list(range(at + 1)) for at in range(count)]


def forward_messages(messages, marker, count):
    if count == 4:
        ahead, marker = lax.optimization_barrier((messages[1], marker))
        return [*messages, send(ahead, [(2, 3)])], marker
    for step in range(2, count):
        pairs = [(at, at + 1) for at in range(step - 1, count - 1)]
        messages = [*messages, send(messages[-1], pairs)]
    return messages, marker


def cost(flops):
    return pl.CostEstimate(flops=flops, bytes_accessed=2**20, transcendentals=0)


def attend(queries, keys, values, conv_kernel, head_mix, norm_gain, bounds):
    rows = queries.shape[0]
    kv, _ = head_mix.shape[:2]
    width = keys.shape[1] // kv
    heads, q_taps, k_taps = conv_kernel.shape
    count = lax.axis_size("ctx")
    dims = (rows, heads, kv, width, q_taps, k_taps)
    f32, bf16 = jnp.float32, jnp.bfloat16
    params = pltpu.CompilerParams(vmem_limit_bytes=28 * 2**20)

    columns = kv * width
    taps_in = conv_kernel.transpose(1, 0, 2)
    queries, keys, values, taps_in = (
        pltpu.with_memory_space_constraint(value, pltpu.HBM)
        for value in (queries, keys, values, taps_in)
    )
    edges, own = pl.pallas_call(
        functools.partial(pack_kernel, dims),
        name="pack",
        out_shape=(
            pltpu.VMEM((HALO, heads * width + columns), bf16),
            pltpu.VMEM((2 * rows, columns), bf16),
        ),
        in_specs=[HBM, HBM, HBM],
        out_specs=(VMEM, VMEM),
        scratch_shapes=[pltpu.SemaphoreType.DMA((4,))],
        compiler_params=params,
    )(queries, keys, values)
    edges = send(edges, [(at, at + 1) for at in range(count - 1)])
    messages, routes = spread_messages(own, count)

    def scratch(extra):
        return [
            pltpu.VMEM((kv, 2 * LANES, rows // BLOCK * width), bf16),
            pltpu.VMEM((2 * (rows + extra), q_taps * width), bf16),
            pltpu.VMEM((2 * (rows + extra), q_taps * width), bf16),
            pltpu.VMEM((rows + extra, rows), f32),
            pltpu.VMEM((rows + extra, rows), f32),
            pltpu.VMEM((rows + extra, columns), bf16),
        ]

    state = [
        pltpu.VMEM((heads, rows), f32),
        pltpu.VMEM((heads, rows), f32),
        pltpu.VMEM((heads, width, rows), f32),
    ]
    deltas = q_taps + k_taps - 1
    qcat, taps, top, total, acc, corner = pl.pallas_call(
        functools.partial(own_kernel, dims),
        name="own_shard",
        out_shape=(
            pltpu.VMEM((heads, rows, q_taps * width), bf16),
            pltpu.VMEM((heads, q_taps * BLOCK, 2 * LANES), bf16),
            *state,
            pltpu.VMEM((heads, 2 * HALO, LANES), f32),
        ),
        in_specs=[HBM, VMEM, VMEM, HBM],
        out_specs=(VMEM,) * 6,
        scratch_shapes=[
            pltpu.VMEM((rows, heads * width), bf16),
            pltpu.VMEM((q_taps, heads, k_taps), f32),
            pltpu.VMEM((q_taps * 16, LANES), f32),
            pltpu.VMEM((rows + HALO, width), f32),
            *scratch(0)[:3],
            pltpu.VMEM((heads, rows, rows), f32),
            pltpu.VMEM((rows, columns), bf16),
            pltpu.VMEM((deltas, rows + HALO + 16, LANES), f32),
            pltpu.VMEM((rows + 2 * HALO, LANES), f32),
            pltpu.VMEM((rows + HALO, LANES), f32),
            pltpu.SemaphoreType.DMA((2,)),
        ],
        compiler_params=params,
        cost_estimate=cost(6 * 10**9),
    )(queries, own, edges, taps_in)
    messages, corner = forward_messages(messages, corner, count)
    for step in range(1, count):
        reads = needed(routes, step, count)
        top, total, acc = pl.pallas_call(
            functools.partial(step_kernel, dims, step, count, routes),
            name="shard_step",
            out_shape=tuple(state),
            in_specs=[VMEM] * (6 + len(reads)),
            out_specs=(VMEM,) * 3,
            scratch_shapes=scratch(HALO if step == count - 1 else 0),
            input_output_aliases={3: 0, 4: 1, 5: 2},
            compiler_params=params,
            cost_estimate=cost(5 * 10**9),
        )(qcat, taps, corner, top, total, acc, *(messages[i] for i in reads))
    return pl.pallas_call(
        functools.partial(final_kernel, dims),
        name="finish",
        out_shape=jax.ShapeDtypeStruct((rows, heads * width), bf16),
        in_specs=[VMEM] * 3 + [SMEM] * 2,
        out_specs=VMEM,
        compiler_params=params,
    )(total, acc, norm_gain.reshape(1, -1), head_mix, bounds)


def solution(mesh):
    return jax.shard_map(
        attend,
        mesh=mesh,
        in_specs=(
            P(("groups", "ctx"), "heads"),
            P(("groups", "ctx"), "heads"),
            P(("groups", "ctx"), "heads"),
            P("heads", None, None),
            P("heads", None, None),
            P("heads"),
            P("groups"),
        ),
        out_specs=P(("groups", "ctx"), "heads"),
        check_vma=False,
    )
```

```python
import functools

import jax
import jax.numpy as jnp
from jax import lax
from jax.experimental import pallas as pl
from jax.experimental.pallas import tpu as pltpu
from jax.sharding import PartitionSpec as P

EPSILON = 1e-06
NEG_FILL = -1e30
LANES = 128
HALO = 16
BLOCK = 64
SLOT = 16


def dot(a, b):
    return jnp.dot(a, b, preferred_element_type=jnp.float32)


def dot_nt(a, b):
    return lax.dot_general(a, b, (((1,), (1,)), ((), ())), preferred_element_type=jnp.float32)


def dot_tn(a, b, precision=None):
    return lax.dot_general(
        a, b, (((0,), (0,)), ((), ())), precision=precision, preferred_element_type=jnp.float32
    )


def split(value):
    high = value.astype(jnp.bfloat16)
    return high, (value - high.astype(jnp.float32)).astype(jnp.bfloat16)


def slot_lane(h):
    return 2 * SLOT * (h % 4) + SLOT * (h // 4)


def fill_windows(rhs, body, after, dims):
    rows, _, kv, width, _, _ = dims
    for g in range(kv):
        cols = slice(g * width, (g + 1) * width)
        for blk in range(rows // BLOCK):
            at = slice(blk * width, (blk + 1) * width)
            first, last = blk * BLOCK, blk * BLOCK + LANES
            if last <= rows:
                piece = body[first:last, cols]
            elif after is None:
                piece = jnp.concatenate(
                    [body[first:rows, cols], jnp.zeros((last - rows, width), jnp.bfloat16)], 0
                )
            else:
                piece = jnp.concatenate([body[first:rows, cols], after[: last - rows, cols]], 0)
            rhs[g, :LANES, at] = piece
            rhs[g, LANES:, at] = piece


def fold_keys(kp, taps, rhs, h, g, dims):
    rows, _, _, width, q_taps, _ = dims
    pair = 2 * width
    for half in range(rows // BLOCK // 2):
        out = dot(taps[h], rhs[g, :, half * pair : (half + 1) * pair])
        for a in range(q_taps):
            for i in range(2):
                piece = out[a * BLOCK : (a + 1) * BLOCK, i * width : (i + 1) * width]
                high, low = split(piece)
                at = (2 * half + i) * BLOCK
                kp[at : at + BLOCK, a * width : (a + 1) * width] = high
                kp[rows + at : rows + at + BLOCK, a * width : (a + 1) * width] = low


def fill_values(vals, body, after, dims):
    rows = dims[0]
    vals[: rows - HALO] = body[rows + HALO :]
    if after is None:
        vals[rows - HALO : rows] = jnp.zeros((HALO, vals.shape[1]), jnp.bfloat16)
    else:
        vals[rows - HALO : rows] = after[rows : rows + HALO]


def first_window(kv_ref, g, width):
    cols = slice(g * width, (g + 1) * width)
    zeros = jnp.zeros((HALO, width), jnp.bfloat16)
    rest = jnp.zeros((LANES - 3 * HALO, width), jnp.bfloat16)
    window = jnp.concatenate([zeros, kv_ref[: 2 * HALO, cols], rest], 0)
    return jnp.concatenate([window, window], 0)


def first_folded(taps_ref, window, h, q_taps):
    taps = jnp.concatenate(
        [taps_ref[h, a * BLOCK : a * BLOCK + HALO] for a in range(q_taps)], 0
    )
    folded = dot(taps, window)
    folded = jnp.concatenate([folded[a * HALO : (a + 1) * HALO] for a in range(q_taps)], 1)
    return jnp.concatenate(split(folded), 0)


def update(scores, values, at, h, m_in, l_in, acc_in, m_ref, l_ref, acc_ref):
    old = m_in[h : h + 1, :]
    top = jnp.maximum(old, jnp.max(scores, axis=0, keepdims=True))
    weights = jnp.exp(scores - top)
    decay = jnp.exp(old - top)
    m_ref[h : h + 1, :] = top
    l_ref[h : h + 1, :] = l_in[h : h + 1, :] * decay + jnp.sum(weights, axis=0, keepdims=True)
    acc_ref[h] = acc_in[h] * decay + dot_tn(values[:, at], weights.astype(jnp.bfloat16))


def pack_kernel(dims, q_hbm, k_hbm, v_hbm, e_ref, kv_ref, sems):
    rows, heads, _, width, _, _ = dims
    qcols = heads * width
    copies = [
        pltpu.make_async_copy(src, dst, sems.at[i])
        for i, (src, dst) in enumerate(
            (
                (q_hbm.at[rows - HALO :], e_ref.at[:, :qcols]),
                (k_hbm.at[rows - HALO :], e_ref.at[:, qcols:]),
                (k_hbm, kv_ref.at[:rows]),
                (v_hbm, kv_ref.at[rows:]),
            )
        )
    ]
    for copy in copies:
        copy.start()
    for copy in copies:
        copy.wait()


def own_kernel(
    dims,
    q_hbm, kv_ref, e_ref, conv_hbm,
    qcat_ref, taps_ref, m_ref, l_ref, acc_ref, corner_ref,
    q_ref, conv, coef, qf, rhs, kp0, kp1, sc, vals, rolled, zband, packed_ref, sems,
):
    rows, heads, kv, width, q_taps, k_taps = dims
    per = heads // kv
    k_edge = k_taps // 2
    qcols = heads * width
    copies = [
        pltpu.make_async_copy(src, dst, sems.at[i])
        for i, (src, dst) in enumerate(
            ((conv_hbm, conv), (q_hbm, q_ref))
        )
    ]
    for copy in copies:
        copy.start()
    scale = width ** (-0.5)
    copies[0].wait()
    fill_windows(rhs, kv_ref, None, dims)
    fill_values(vals, kv_ref, None, dims)
    lane8 = lax.broadcasted_iota(jnp.int32, (heads, LANES), 1)
    bases = []
    owner = lane8 // (2 * SLOT) + 4 * ((lane8 // SLOT) % 2)
    spread = jnp.where(
        owner == lax.broadcasted_iota(jnp.int32, (heads, LANES), 0), 1.0, 0.0
    ).astype(jnp.float32)
    offset = lax.broadcasted_iota(jnp.int32, (k_taps, LANES), 1) % SLOT
    tap = lax.broadcasted_iota(jnp.int32, (k_taps, LANES), 0)
    reach = q_taps - 1 + k_edge
    for a in range(q_taps):
        weights = conv[a] * scale
        base = jnp.zeros((heads, LANES), jnp.float32)
        for t in range(k_taps):
            base = jnp.where(lane8 == HALO + k_edge - t, weights[:, t : t + 1], base)
        bases.append(base)
        lanes = dot_tn(weights, spread, lax.Precision.HIGHEST)
        source = offset + tap - k_edge - a
        inside = (source >= 0) & (source < SLOT) & (offset < reach)
        coef[a * 16 : a * 16 + k_taps] = jnp.where(inside, lanes, 0.0)
    copies[1].wait()
    blocks = rows // LANES
    tall = rows + HALO
    lane = lax.broadcasted_iota(jnp.int32, (tall, LANES), 1)
    sub = lax.broadcasted_iota(jnp.int32, (tall, LANES), 0)
    lane_small = lax.broadcasted_iota(jnp.int32, (HALO, LANES), 1)
    packs = [jnp.zeros((tall, LANES), jnp.float32) for _ in range(2)]
    for h in range(heads):
        g = h // per
        cols = slice(h * width, (h + 1) * width)
        kcols = slice(g * width, (g + 1) * width)
        for a in range(q_taps):
            tile = pltpu.roll(
                jnp.broadcast_to(bases[a][h : h + 1], (BLOCK, LANES)),
                0, 1, stride=1, stride_axis=0,
            )
            high, low = split(tile)
            taps_ref[h, a * BLOCK : (a + 1) * BLOCK, :LANES] = high
            taps_ref[h, a * BLOCK : (a + 1) * BLOCK, LANES:] = low
        qf[:HALO] = e_ref[:, cols].astype(jnp.float32)
        qf[HALO:] = q_ref[:, cols].astype(jnp.float32)
        qcat_ref[h, :, :width] = q_ref[:, cols]
        for a in range(1, q_taps):
            qcat_ref[h, :, a * width : (a + 1) * width] = qf[
                HALO - a : HALO - a + rows
            ].astype(jnp.bfloat16)
        near = jnp.concatenate([q_ref[: LANES - HALO, cols], e_ref[:, cols]], 0)
        pieces = [dot_nt(e_ref[:, qcols + g * width : qcols + (g + 1) * width], near)]
        for blk in range(blocks):
            key_blk = kv_ref[blk * LANES : (blk + 1) * LANES, kcols]
            last = min(rows, (blk + 2) * LANES)
            raw = dot_nt(key_blk, q_ref[blk * LANES : last, cols])
            if last == (blk + 2) * LANES:
                pieces.append(raw[: LANES - HALO, :LANES])
                pieces.append(
                    jnp.where(
                        lane_small < LANES // 2,
                        raw[LANES - HALO :, LANES:],
                        raw[LANES - HALO :, :LANES],
                    )
                )
            else:
                pieces.append(raw)
        ring = jnp.concatenate(pieces, 0)
        moved = []
        for first in range(0, tall, 8):
            shift = (slot_lane(h) + HALO - first) % LANES
            part = ring[first : first + 8]
            moved.append(pltpu.roll(part, shift, 1) if shift else part)
        mine = (lane - slot_lane(h)) % LANES < 2 * SLOT
        packs[h // 4] = jnp.where(mine, jnp.concatenate(moved, 0), packs[h // 4])
    for i in range(2 if heads > 4 else 1):
        for bit in (1, 2, 4):
            packs[i] = jnp.where(
                (sub & bit) != 0, pltpu.roll(packs[i], LANES - bit, 1), packs[i]
            )
    packed_ref[...] = jnp.where((lane // SLOT) % 2 == 0, packs[0], packs[1])
    deltas = list(enumerate(range(-k_edge - q_taps + 1, k_edge + 1)))

    def roll_unit(order, delta):
        rolled[order, :8] = jnp.zeros((8, LANES), jnp.float32)
        shift = (-delta) % LANES
        value = packed_ref[...]
        rolled[order, 8 : 8 + tall] = pltpu.roll(value, shift, 1) if shift else value
        rolled[order, 8 + tall :] = jnp.zeros((8, LANES), jnp.float32)

    def band_unit(first):
        total = jnp.zeros((HALO, LANES), jnp.float32)
        for order, delta in deltas:
            for a in range(q_taps):
                t = k_edge + a + delta
                if 0 <= t < k_taps:
                    at = 8 + first + k_edge - t
                    row = a * 16 + t
                    total = total + coef[row : row + 1, :] * rolled[order, at : at + HALO]
        zband[first : first + HALO] = total

    units = [functools.partial(roll_unit, *pair) for pair in deltas]
    units += [functools.partial(band_unit, first) for first in range(0, tall, HALO)]
    zband[tall:] = jnp.zeros((HALO, LANES), jnp.float32)
    key_id = HALO + lax.broadcasted_iota(jnp.int32, (rows, rows), 0)
    row_id = lax.broadcasted_iota(jnp.int32, (rows, rows), 1)

    def finish_head(h):
        g = h // per
        base = slot_lane(h)
        corner_ref[h] = pltpu.roll(
            zband[: 2 * HALO], (LANES - HALO - base) % LANES, 1, stride=1, stride_axis=0
        )
        strips = []
        for blk in range(blocks):
            at = 2 * HALO + blk * LANES
            tile = pltpu.roll(
                zband[at : at + LANES], (HALO - base) % LANES, 1, stride=1, stride_axis=0
            )
            strips.append(jnp.concatenate([tile] * blocks, 1))
        exact = jnp.concatenate(strips, 0)
        scores = jnp.where(row_id - key_id < reach, exact, sc[h])
        scores = jnp.where(key_id <= row_id, scores, NEG_FILL)
        top = jnp.max(scores, axis=0, keepdims=True)
        weights = jnp.where(key_id <= row_id, jnp.exp(scores - top), 0.0)
        m_ref[h : h + 1, :] = top
        l_ref[h : h + 1, :] = jnp.sum(weights, axis=0, keepdims=True)
        acc_ref[h] = dot_tn(vals[:, g * width : (g + 1) * width], weights.astype(jnp.bfloat16))

    kps = (kp0, kp1)
    early = max(1, heads - 3)
    share = -(-len(units) // early)
    done = 0
    for h in range(heads):
        fold_keys(kps[h % 2], taps_ref, rhs, h, h // per, dims)
        if h < early:
            for unit in units[h * share : (h + 1) * share]:
                unit()
        else:
            for _ in range(2):
                if done < h:
                    finish_head(done)
                    done += 1
        both = dot_nt(kps[h % 2][...], qcat_ref[h])
        sc[h] = both[:rows] + both[rows:]
    for h in range(done, heads):
        finish_head(h)


def first_positions(dims, place, qcat_ref, taps_ref, kv_ref, corner_ref, state_in, state):
    rows, heads, kv, width, q_taps, k_taps = dims
    per = heads // kv
    reach = q_taps - 1 + k_taps // 2
    key_id = lax.broadcasted_iota(jnp.int32, (HALO, rows), 0)
    row_id = place * rows + lax.broadcasted_iota(jnp.int32, (HALO, rows), 1)
    for g in range(kv):
        window = first_window(kv_ref, g, width)
        at = slice(g * width, (g + 1) * width)
        for h in range(g * per, (g + 1) * per):
            both = dot_nt(first_folded(taps_ref, window, h, q_taps), qcat_ref[h])
            scores = both[:HALO] + both[HALO:]
            exact = jnp.concatenate([corner_ref[h, HALO:]] * (rows // LANES), 1)
            scores = jnp.where(row_id - key_id < reach, exact, scores)
            scores = jnp.where(key_id <= row_id, scores, NEG_FILL)
            update(scores, kv_ref.at[rows : rows + HALO], at, h, *state_in, *state)


def needed(routes, step, count):
    reads = {routes[at][step - i] for at in range(step, count) for i in range(2)}
    if step == count - 1:
        reads |= {routes[at][at] for at in range(step)}
    return sorted(reads)


def step_kernel(dims, step, count, routes, qcat_ref, taps_ref, corner_ref, m_in, l_in, acc_in, *rest):
    rows, heads, kv, width, q_taps, k_taps = dims
    per = heads // kv
    reach = q_taps - 1 + k_taps // 2
    final = step == count - 1
    messages = dict(zip(needed(routes, step, count), rest[:-9]))
    m_ref, l_ref, acc_ref, rhs, kp0, kp1, sc0, sc1, vals = rest[-9:]
    place = lax.axis_index("ctx")
    states = (m_in, l_in, acc_in), (m_ref, l_ref, acc_ref)

    @pl.when(place >= step)
    def _():
        pairs = [(routes[at][step], routes[at][step - 1]) for at in range(step, count)]
        for pair in sorted(set(pairs)):
            here = [step + i for i, other in enumerate(pairs) if other == pair]

            def load(body=messages[pair[0]], after=messages[pair[1]]):
                fill_windows(rhs, body, after, dims)
                fill_values(vals, body, after, dims)

            if len(here) == len(pairs):
                load()
            else:
                pl.when(functools.reduce(jnp.logical_or, [place == at for at in here]))(load)
        body = messages[routes[count - 1][step]]
        if final:
            vals[rows:] = body[rows : rows + HALO]
        key_id = lax.broadcasted_iota(jnp.int32, (2 * HALO, LANES), 0) - HALO
        row_id = lax.broadcasted_iota(jnp.int32, (2 * HALO, LANES), 1)
        kps, scs = (kp0, kp1), (sc0, sc1)

        def fold(h):
            fold_keys(kps[h % 2], taps_ref, rhs, h, h // per, dims)
            if final:
                window = first_window(body, h // per, width)
                kps[h % 2][2 * rows :] = first_folded(taps_ref, window, h, q_taps)

        fold(0)
        for h in range(heads):
            g = h // per
            sc = scs[h % 2]
            both = dot_nt(kps[h % 2][...], qcat_ref[h])
            sc[:rows] = both[:rows] + both[rows : 2 * rows]
            if final:
                sc[rows:] = both[2 * rows : 2 * rows + HALO] + both[2 * rows + HALO :]
            if h + 1 < heads:
                fold(h + 1)
            if step == 1:
                at = slice(rows - 2 * HALO, rows)
                patch = sc[at, :LANES]
                patch = jnp.where(row_id - key_id < reach, corner_ref[h], patch)
                sc[at, :LANES] = jnp.where(key_id <= row_id, patch, NEG_FILL)
            at = slice(g * width, (g + 1) * width)
            update(sc[...], vals, at, h, *states[0], *states[1])

    if final:
        for at in range(step):
            @pl.when(place == at)
            def _(at=at):
                first_positions(
                    dims, place, qcat_ref, taps_ref, messages[routes[at][at]], corner_ref, *states
                )


def final_kernel(dims, l_ref, acc_ref, gain_ref, mix_ref, bounds_ref, o_ref):
    rows, heads, kv, width, _, _ = dims
    per = heads // kv
    row_pos = lax.axis_index("ctx") * rows + lax.broadcasted_iota(jnp.int32, (rows, 1), 0)
    live = (row_pos >= bounds_ref[0]) & (row_pos < bounds_ref[1])
    for g in range(kv):
        probs = [acc_ref[h] * (1.0 / l_ref[h : h + 1, :]) for h in range(g * per, (g + 1) * per)]
        for a in range(per):
            blended = mix_ref[g, a, 0] * probs[0]
            for b in range(1, per):
                blended = blended + mix_ref[g, a, b] * probs[b]
            mean_sq = jnp.mean(blended * blended, axis=0, keepdims=True)
            normed = (blended * lax.rsqrt(mean_sq + EPSILON)).T
            h = g * per + a
            normed = normed * gain_ref[:, h * width : (h + 1) * width]
            o_ref[:, h * width : (h + 1) * width] = jnp.where(live, normed, 0.0).astype(jnp.bfloat16)


VMEM = pl.BlockSpec(memory_space=pltpu.VMEM)
SMEM = pl.BlockSpec(memory_space=pltpu.SMEM)
HBM = pl.BlockSpec(memory_space=pltpu.HBM)


def send(value, pairs):
    return lax.ppermute(value, "ctx", pairs)


def spread_messages(own, count):
    if count == 4:
        first = send(own, [(0, 1), (1, 2), (2, 3)])
        second = send(own, [(0, 2)])
        return [own, first, second], [[0], [0, 1], [0, 1, 2], [0, 1, 3, 4]]
    first = send(own, [(at, at + 1) for at in range(count - 1)])
    return [own, first], [list(range(at + 1)) for at in range(count)]


def forward_messages(messages, marker, count, stage):
    if count != 4:
        chain = range(2, count) if stage == 0 else ()
        for step in chain:
            pairs = [(at, at + 1) for at in range(step - 1, count - 1)]
            messages = [*messages, send(messages[-1], pairs)]
    elif stage < 2:
        source, marker = lax.optimization_barrier((messages[stage + 1], marker))
        messages = [*messages, send(source, [(2, 3)])]
    return messages, marker


def cost(flops):
    return pl.CostEstimate(flops=flops, bytes_accessed=2**20, transcendentals=0)


def attend(queries, keys, values, conv_kernel, head_mix, norm_gain, bounds):
    rows = queries.shape[0]
    kv, _ = head_mix.shape[:2]
    width = keys.shape[1] // kv
    heads, q_taps, k_taps = conv_kernel.shape
    count = lax.axis_size("ctx")
    dims = (rows, heads, kv, width, q_taps, k_taps)
    f32, bf16 = jnp.float32, jnp.bfloat16
    params = pltpu.CompilerParams(vmem_limit_bytes=28 * 2**20)

    columns = kv * width
    taps_in = conv_kernel.transpose(1, 0, 2)
    queries, keys, values, taps_in = (
        pltpu.with_memory_space_constraint(value, pltpu.HBM)
        for value in (queries, keys, values, taps_in)
    )
    edges, own = pl.pallas_call(
        functools.partial(pack_kernel, dims),
        name="pack",
        out_shape=(
            pltpu.VMEM((HALO, heads * width + columns), bf16),
            pltpu.VMEM((2 * rows, columns), bf16),
        ),
        in_specs=[HBM, HBM, HBM],
        out_specs=(VMEM, VMEM),
        scratch_shapes=[pltpu.SemaphoreType.DMA((4,))],
        compiler_params=params,
    )(queries, keys, values)
    edges = send(edges, [(at, at + 1) for at in range(count - 1)])
    messages, routes = spread_messages(own, count)

    def scratch(extra):
        return [
            pltpu.VMEM((kv, 2 * LANES, rows // BLOCK * width), bf16),
            pltpu.VMEM((2 * (rows + extra), q_taps * width), bf16),
            pltpu.VMEM((2 * (rows + extra), q_taps * width), bf16),
            pltpu.VMEM((rows + extra, rows), f32),
            pltpu.VMEM((rows + extra, rows), f32),
            pltpu.VMEM((rows + extra, columns), bf16),
        ]

    state = [
        pltpu.VMEM((heads, rows), f32),
        pltpu.VMEM((heads, rows), f32),
        pltpu.VMEM((heads, width, rows), f32),
    ]
    deltas = q_taps + k_taps - 1
    qcat, taps, top, total, acc, corner = pl.pallas_call(
        functools.partial(own_kernel, dims),
        name="own_shard",
        out_shape=(
            pltpu.VMEM((heads, rows, q_taps * width), bf16),
            pltpu.VMEM((heads, q_taps * BLOCK, 2 * LANES), bf16),
            *state,
            pltpu.VMEM((heads, 2 * HALO, LANES), f32),
        ),
        in_specs=[HBM, VMEM, VMEM, HBM],
        out_specs=(VMEM,) * 6,
        scratch_shapes=[
            pltpu.VMEM((rows, heads * width), bf16),
            pltpu.VMEM((q_taps, heads, k_taps), f32),
            pltpu.VMEM((q_taps * 16, LANES), f32),
            pltpu.VMEM((rows + HALO, width), f32),
            *scratch(0)[:3],
            pltpu.VMEM((heads, rows, rows), f32),
            pltpu.VMEM((rows, columns), bf16),
            pltpu.VMEM((deltas, rows + HALO + 16, LANES), f32),
            pltpu.VMEM((rows + 2 * HALO, LANES), f32),
            pltpu.VMEM((rows + HALO, LANES), f32),
            pltpu.SemaphoreType.DMA((2,)),
        ],
        compiler_params=params,
        cost_estimate=cost(6 * 10**9),
    )(queries, own, edges, taps_in)
    messages, corner = forward_messages(messages, corner, count, 0)
    for step in range(1, count):
        reads = needed(routes, step, count)
        top, total, acc = pl.pallas_call(
            functools.partial(step_kernel, dims, step, count, routes),
            name="shard_step",
            out_shape=tuple(state),
            in_specs=[VMEM] * (6 + len(reads)),
            out_specs=(VMEM,) * 3,
            scratch_shapes=scratch(HALO if step == count - 1 else 0),
            input_output_aliases={3: 0, 4: 1, 5: 2},
            compiler_params=params,
            cost_estimate=cost(5 * 10**9),
        )(qcat, taps, corner, top, total, acc, *(messages[i] for i in reads))
        messages, top = forward_messages(messages, top, count, step)
    return pl.pallas_call(
        functools.partial(final_kernel, dims),
        name="finish",
        out_shape=jax.ShapeDtypeStruct((rows, heads * width), bf16),
        in_specs=[VMEM] * 3 + [SMEM] * 2,
        out_specs=VMEM,
        compiler_params=params,
    )(total, acc, norm_gain.reshape(1, -1), head_mix, bounds)


def solution(mesh):
    return jax.shard_map(
        attend,
        mesh=mesh,
        in_specs=(
            P(("groups", "ctx"), "heads"),
            P(("groups", "ctx"), "heads"),
            P(("groups", "ctx"), "heads"),
            P("heads", None, None),
            P("heads", None, None),
            P("heads"),
            P("groups"),
        ),
        out_specs=P(("groups", "ctx"), "heads"),
        check_vma=False,
    )
```

```python
import functools

import jax
import jax.numpy as jnp
from jax import lax
from jax.experimental import pallas as pl
from jax.experimental.pallas import tpu as pltpu
from jax.sharding import PartitionSpec as P

EPSILON = 1e-06
NEG_FILL = -1e30
LANES = 128
HALO = 16
BLOCK = 64
SLOT = 16
FOLD_TAPS = 2


def dot(a, b):
    return jnp.dot(a, b, preferred_element_type=jnp.float32)


def dot_nt(a, b):
    return lax.dot_general(a, b, (((1,), (1,)), ((), ())), preferred_element_type=jnp.float32)


def dot_tn(a, b, precision=None):
    return lax.dot_general(
        a, b, (((0,), (0,)), ((), ())), precision=precision, preferred_element_type=jnp.float32
    )


def split(value):
    high = value.astype(jnp.bfloat16)
    return high, (value - high.astype(jnp.float32)).astype(jnp.bfloat16)


def slot_lane(h):
    return 2 * SLOT * (h % 4) + SLOT * (h // 4)


def fill_group(rhs, vals, g, body, after, dims):
    rows, _, _, width, _, _ = dims
    cols = slice(g * width, (g + 1) * width)
    for blk in range(rows // BLOCK):
        at = slice(blk * width, (blk + 1) * width)
        first, last = blk * BLOCK, blk * BLOCK + LANES
        if last <= rows:
            piece = body[first:last, cols]
        elif after is None:
            piece = jnp.concatenate(
                [body[first:rows, cols], jnp.zeros((last - rows, width), jnp.bfloat16)], 0
            )
        else:
            piece = jnp.concatenate([body[first:rows, cols], after[: last - rows, cols]], 0)
        rhs[g, :LANES, at] = piece
        rhs[g, LANES:, at] = piece
    vals[: rows - HALO, cols] = body[rows + HALO :, cols]
    if after is None:
        vals[rows - HALO : rows, cols] = jnp.zeros((HALO, width), jnp.bfloat16)
    else:
        vals[rows - HALO : rows, cols] = after[rows : rows + HALO, cols]


def fold_keys(kp, taps, rhs, h, g, dims):
    rows, _, _, width, q_taps, _ = dims
    for first in range(0, q_taps, FOLD_TAPS):
        last = min(q_taps, first + FOLD_TAPS)
        out = dot(taps[h, first * BLOCK : last * BLOCK], rhs[g])
        for a in range(first, last):
            for blk in range(rows // BLOCK):
                at, row = blk * BLOCK, (a - first) * BLOCK
                high, low = split(out[row : row + BLOCK, blk * width : (blk + 1) * width])
                kp[at : at + BLOCK, a * width : (a + 1) * width] = high
                kp[rows + at : rows + at + BLOCK, a * width : (a + 1) * width] = low


def first_window(kv_ref, g, width):
    cols = slice(g * width, (g + 1) * width)
    zeros = jnp.zeros((HALO, width), jnp.bfloat16)
    rest = jnp.zeros((LANES - 3 * HALO, width), jnp.bfloat16)
    window = jnp.concatenate([zeros, kv_ref[: 2 * HALO, cols], rest], 0)
    return jnp.concatenate([window, window], 0)


def first_folded(taps_ref, window, h, q_taps):
    taps = jnp.concatenate(
        [taps_ref[h, a * BLOCK : a * BLOCK + HALO] for a in range(q_taps)], 0
    )
    folded = dot(taps, window)
    folded = jnp.concatenate([folded[a * HALO : (a + 1) * HALO] for a in range(q_taps)], 1)
    return jnp.concatenate(split(folded), 0)


def update(scores, values, at, h, m_in, l_in, acc_in, m_ref, l_ref, acc_ref):
    old = m_in[h : h + 1, :]
    top = jnp.maximum(old, jnp.max(scores, axis=0, keepdims=True))
    weights = jnp.exp(scores - top)
    decay = jnp.exp(old - top)
    m_ref[h : h + 1, :] = top
    l_ref[h : h + 1, :] = l_in[h : h + 1, :] * decay + jnp.sum(weights, axis=0, keepdims=True)
    acc_ref[h] = acc_in[h] * decay + dot_tn(values[:, at], weights.astype(jnp.bfloat16))


def pack_kernel(dims, q_hbm, k_hbm, v_hbm, e_ref, kv_ref, sems):
    rows, heads, _, width, _, _ = dims
    qcols = heads * width
    moves = (
        (q_hbm.at[rows - HALO :], e_ref.at[:, :qcols]),
        (k_hbm.at[rows - HALO :], e_ref.at[:, qcols:]),
        (k_hbm, kv_ref.at[:rows]),
        (v_hbm, kv_ref.at[rows:]),
    )
    copies = [pltpu.make_async_copy(*move, sems.at[i]) for i, move in enumerate(moves)]
    for copy in copies:
        copy.start()
    for copy in copies:
        copy.wait()


def taps_kernel(dims, conv_hbm, taps_ref, coef_ref, conv, sem):
    _, heads, _, width, q_taps, k_taps = dims
    k_edge = k_taps // 2
    copy = pltpu.make_async_copy(conv_hbm, conv, sem)
    copy.start()
    copy.wait()
    lane = lax.broadcasted_iota(jnp.int32, (heads, LANES), 1)
    owner = lane // (2 * SLOT) + 4 * ((lane // SLOT) % 2)
    spread = jnp.where(
        owner == lax.broadcasted_iota(jnp.int32, (heads, LANES), 0), 1.0, 0.0
    ).astype(jnp.float32)
    offset = lax.broadcasted_iota(jnp.int32, (k_taps, LANES), 1) % SLOT
    tap = lax.broadcasted_iota(jnp.int32, (k_taps, LANES), 0)
    for a in range(q_taps):
        weights = conv[a] * width ** (-0.5)
        base = jnp.zeros((heads, LANES), jnp.float32)
        for t in range(k_taps):
            base = jnp.where(lane == HALO + k_edge - t, weights[:, t : t + 1], base)
        for h in range(heads):
            tile = pltpu.roll(
                jnp.broadcast_to(base[h : h + 1], (BLOCK, LANES)), 0, 1, stride=1, stride_axis=0
            )
            high, low = split(tile)
            taps_ref[h, a * BLOCK : (a + 1) * BLOCK, :LANES] = high
            taps_ref[h, a * BLOCK : (a + 1) * BLOCK, LANES:] = low
        lanes = dot_tn(weights, spread, lax.Precision.HIGHEST)
        source = offset + tap - k_edge - a
        inside = (source >= 0) & (source < SLOT) & (offset < q_taps - 1 + k_edge)
        coef_ref[a * 16 : a * 16 + k_taps] = jnp.where(inside, lanes, 0.0)


def own_kernel(
    dims,
    q_hbm, kv_ref, e_ref, taps_ref, coef,
    qcat_ref, m_ref, l_ref, acc_ref, corner_ref,
    q_ref, qf, rhs, kp0, kp1, sc, vals, rolled, zband, packed_ref, sem,
):
    rows, heads, kv, width, q_taps, k_taps = dims
    per = heads // kv
    k_edge = k_taps // 2
    reach = q_taps - 1 + k_edge
    qcols = heads * width
    copy = pltpu.make_async_copy(q_hbm, q_ref, sem)
    copy.start()
    for g in range(kv):
        fill_group(rhs, vals, g, kv_ref, None, dims)
    copy.wait()
    blocks = rows // LANES
    tall = rows + HALO
    lane = lax.broadcasted_iota(jnp.int32, (tall, LANES), 1)
    sub = lax.broadcasted_iota(jnp.int32, (tall, LANES), 0)
    lane_small = lax.broadcasted_iota(jnp.int32, (HALO, LANES), 1)
    packs = [jnp.zeros((tall, LANES), jnp.float32) for _ in range(2)]
    for h in range(heads):
        g = h // per
        cols = slice(h * width, (h + 1) * width)
        kcols = slice(g * width, (g + 1) * width)
        qf[:HALO] = e_ref[:, cols].astype(jnp.float32)
        qf[HALO:] = q_ref[:, cols].astype(jnp.float32)
        qcat_ref[h, :, :width] = q_ref[:, cols]
        for a in range(1, q_taps):
            qcat_ref[h, :, a * width : (a + 1) * width] = qf[
                HALO - a : HALO - a + rows
            ].astype(jnp.bfloat16)
        near = jnp.concatenate([q_ref[: LANES - HALO, cols], e_ref[:, cols]], 0)
        pieces = [dot_nt(e_ref[:, qcols + g * width : qcols + (g + 1) * width], near)]
        for blk in range(blocks):
            key_blk = kv_ref[blk * LANES : (blk + 1) * LANES, kcols]
            last = min(rows, (blk + 2) * LANES)
            raw = dot_nt(key_blk, q_ref[blk * LANES : last, cols])
            if last == (blk + 2) * LANES:
                pieces.append(raw[: LANES - HALO, :LANES])
                pieces.append(
                    jnp.where(
                        lane_small < LANES // 2,
                        raw[LANES - HALO :, LANES:],
                        raw[LANES - HALO :, :LANES],
                    )
                )
            else:
                pieces.append(raw)
        ring = jnp.concatenate(pieces, 0)
        moved = []
        for first in range(0, tall, 8):
            shift = (slot_lane(h) + HALO - first) % LANES
            part = ring[first : first + 8]
            moved.append(pltpu.roll(part, shift, 1) if shift else part)
        mine = (lane - slot_lane(h)) % LANES < 2 * SLOT
        packs[h // 4] = jnp.where(mine, jnp.concatenate(moved, 0), packs[h // 4])
    for i in range(2 if heads > 4 else 1):
        for bit in (1, 2, 4):
            packs[i] = jnp.where(
                (sub & bit) != 0, pltpu.roll(packs[i], LANES - bit, 1), packs[i]
            )
    packed_ref[...] = jnp.where((lane // SLOT) % 2 == 0, packs[0], packs[1])
    deltas = list(enumerate(range(-k_edge - q_taps + 1, k_edge + 1)))

    def roll_unit(order, delta):
        rolled[order, :8] = jnp.zeros((8, LANES), jnp.float32)
        shift = (-delta) % LANES
        value = packed_ref[...]
        rolled[order, 8 : 8 + tall] = pltpu.roll(value, shift, 1) if shift else value
        rolled[order, 8 + tall :] = jnp.zeros((8, LANES), jnp.float32)

    def band_unit(first):
        total = jnp.zeros((HALO, LANES), jnp.float32)
        for order, delta in deltas:
            for a in range(q_taps):
                t = k_edge + a + delta
                if 0 <= t < k_taps:
                    at = 8 + first + k_edge - t
                    row = a * 16 + t
                    total = total + coef[row : row + 1, :] * rolled[order, at : at + HALO]
        zband[first : first + HALO] = total

    units = [functools.partial(roll_unit, *pair) for pair in deltas]
    units += [functools.partial(band_unit, first) for first in range(0, tall, HALO)]
    zband[tall:] = jnp.zeros((HALO, LANES), jnp.float32)
    key_id = HALO + lax.broadcasted_iota(jnp.int32, (rows, rows), 0)
    row_id = lax.broadcasted_iota(jnp.int32, (rows, rows), 1)

    def finish_head(h):
        g = h // per
        base = slot_lane(h)
        corner_ref[h] = pltpu.roll(
            zband[: 2 * HALO], (LANES - HALO - base) % LANES, 1, stride=1, stride_axis=0
        )
        strips = []
        for blk in range(blocks):
            at = 2 * HALO + blk * LANES
            tile = pltpu.roll(
                zband[at : at + LANES], (HALO - base) % LANES, 1, stride=1, stride_axis=0
            )
            strips.append(jnp.concatenate([tile] * blocks, 1))
        exact = jnp.concatenate(strips, 0)
        scores = jnp.where(row_id - key_id < reach, exact, sc[h])
        scores = jnp.where(key_id <= row_id, scores, NEG_FILL)
        top = jnp.max(scores, axis=0, keepdims=True)
        weights = jnp.where(key_id <= row_id, jnp.exp(scores - top), 0.0)
        m_ref[h : h + 1, :] = top
        l_ref[h : h + 1, :] = jnp.sum(weights, axis=0, keepdims=True)
        acc_ref[h] = dot_tn(vals[:, g * width : (g + 1) * width], weights.astype(jnp.bfloat16))

    kps = (kp0, kp1)
    early = max(1, heads - 3)
    share = -(-len(units) // early)
    done = 0
    for h in range(heads):
        fold_keys(kps[h % 2], taps_ref, rhs, h, h // per, dims)
        if h < early:
            for unit in units[h * share : (h + 1) * share]:
                unit()
        else:
            for _ in range(2):
                if done < h:
                    finish_head(done)
                    done += 1
        both = dot_nt(kps[h % 2][...], qcat_ref[h])
        sc[h] = both[:rows] + both[rows:]
    for h in range(done, heads):
        finish_head(h)


def first_positions(dims, qcat_ref, taps_ref, kv_ref, corner_ref, state_in, state):
    rows, heads, kv, width, q_taps, k_taps = dims
    per = heads // kv
    reach = q_taps - 1 + k_taps // 2
    key_id = lax.broadcasted_iota(jnp.int32, (HALO, rows), 0)
    row_id = lax.broadcasted_iota(jnp.int32, (HALO, rows), 1)
    for h in range(heads):
        g = h // per
        both = dot_nt(first_folded(taps_ref, first_window(kv_ref, g, width), h, q_taps), qcat_ref[h])
        scores = both[:HALO] + both[HALO:]
        exact = jnp.concatenate([corner_ref[h, HALO:]] * (rows // LANES), 1)
        scores = jnp.where(row_id - key_id < reach, exact, scores)
        scores = jnp.where(key_id <= row_id, scores, NEG_FILL)
        at = slice(g * width, (g + 1) * width)
        update(scores, kv_ref.at[rows : rows + HALO], at, h, *state_in, *state)


def add_shard(
    dims, step, extra, qcat_ref, taps_ref, corner_ref, body, after, state_in, state, scratch, finish
):
    rows, heads, kv, width, q_taps, k_taps = dims
    per = heads // kv
    reach = q_taps - 1 + k_taps // 2
    rhs, kp0, kp1, sc0, sc1, vals = scratch
    kps, scs = (kp0, kp1), (sc0, sc1)
    total = rows + HALO if extra else rows
    for g in range(kv):
        fill_group(rhs, vals, g, body, after, dims)
    if extra:
        vals[rows:] = body[rows : rows + HALO]
    key_id = lax.broadcasted_iota(jnp.int32, (2 * HALO, LANES), 0) - HALO
    row_id = lax.broadcasted_iota(jnp.int32, (2 * HALO, LANES), 1)

    def fold(h):
        fold_keys(kps[h % 2], taps_ref, rhs, h, h // per, dims)
        if extra:
            window = first_window(body, h // per, width)
            kps[h % 2][2 * rows :] = first_folded(taps_ref, window, h, q_taps)

    fold(0)
    for h in range(heads):
        g = h // per
        sc = scs[h % 2]
        both = dot_nt(kps[h % 2][: 2 * total], qcat_ref[h])
        sc[:rows] = both[:rows] + both[rows : 2 * rows]
        if extra:
            sc[rows:] = both[2 * rows : 2 * rows + HALO] + both[2 * rows + HALO :]
        if h + 1 < heads:
            fold(h + 1)
        if step == 1:
            at = slice(rows - 2 * HALO, rows)
            patch = sc[at, :LANES]
            patch = jnp.where(row_id - key_id < reach, corner_ref[h], patch)
            sc[at, :LANES] = jnp.where(key_id <= row_id, patch, NEG_FILL)
        at = slice(g * width, (g + 1) * width)
        update(sc[:total], vals.at[:total], at, h, *state_in, *state)
        if finish is not None and h % per == per - 1:
            finish(g)


def step_kernel(
    dims, step, qcat_ref, taps_ref, corner_ref, m_in, l_in, acc_in, after, body,
    m_ref, l_ref, acc_ref, *scratch
):
    place = lax.axis_index("ctx")
    states = (m_in, l_in, acc_in), (m_ref, l_ref, acc_ref)
    fixed = (qcat_ref, taps_ref, corner_ref, body, after, *states, scratch, None)

    @pl.when(place == step)
    def _():
        add_shard(dims, step, True, *fixed)

    @pl.when(place > step)
    def _():
        add_shard(dims, step, False, *fixed)


def last_kernel(
    dims, step, qcat_ref, taps_ref, corner_ref, m_in, l_in, acc_in, after, body, own,
    gain_ref, mix_ref, bounds_ref, o_hbm, m_ref, l_ref, acc_ref, out, sems, *scratch
):
    rows, heads, kv, width, _, _ = dims
    per = heads // kv
    place = lax.axis_index("ctx")
    row_pos = place * rows + lax.broadcasted_iota(jnp.int32, (rows, 1), 0)
    live = (row_pos >= bounds_ref[0]) & (row_pos < bounds_ref[1])
    states = (m_in, l_in, acc_in), (m_ref, l_ref, acc_ref)

    def copy_out(g):
        cols = pl.ds(g * per * width, per * width)
        return pltpu.make_async_copy(out.at[:, cols], o_hbm.at[:, cols], sems.at[g])

    def finish(g):
        probs = [acc_ref[h] * (1.0 / l_ref[h : h + 1, :]) for h in range(g * per, (g + 1) * per)]
        for a in range(per):
            blended = mix_ref[g, a, 0] * probs[0]
            for b in range(1, per):
                blended = blended + mix_ref[g, a, b] * probs[b]
            mean_sq = jnp.mean(blended * blended, axis=0, keepdims=True)
            normed = (blended * lax.rsqrt(mean_sq + EPSILON)).T
            at = slice((g * per + a) * width, (g * per + a + 1) * width)
            normed = jnp.where(live, normed * gain_ref[:, at], 0.0)
            out[:, at] = normed.astype(jnp.bfloat16)
        copy_out(g).start()

    @pl.when(place == step)
    def _():
        add_shard(
            dims, step, True, qcat_ref, taps_ref, corner_ref, body, after, *states, scratch, finish
        )

    @pl.when(place < step)
    def _():
        @pl.when(place == 0)
        def _():
            first_positions(dims, qcat_ref, taps_ref, own, corner_ref, *states)

        @pl.when(place > 0)
        def _():
            l_ref[...] = l_in[...]
            acc_ref[...] = acc_in[...]

        for g in range(kv):
            finish(g)

    for g in range(kv):
        copy_out(g).wait()


VMEM = pl.BlockSpec(memory_space=pltpu.VMEM)
SMEM = pl.BlockSpec(memory_space=pltpu.SMEM)
HBM = pl.BlockSpec(memory_space=pltpu.HBM)


def send(value, pairs):
    return lax.ppermute(value, "ctx", pairs)


def cost(flops):
    return pl.CostEstimate(flops=flops, bytes_accessed=2**20, transcendentals=0)


def attend(queries, keys, values, conv_kernel, head_mix, norm_gain, bounds):
    rows = queries.shape[0]
    kv, _ = head_mix.shape[:2]
    width = keys.shape[1] // kv
    heads, q_taps, k_taps = conv_kernel.shape
    count = lax.axis_size("ctx")
    dims = (rows, heads, kv, width, q_taps, k_taps)
    f32, bf16 = jnp.float32, jnp.bfloat16
    params = pltpu.CompilerParams(vmem_limit_bytes=28 * 2**20)

    columns = kv * width
    taps_in = conv_kernel.transpose(1, 0, 2)
    queries, keys, values, taps_in = (
        pltpu.with_memory_space_constraint(value, pltpu.HBM)
        for value in (queries, keys, values, taps_in)
    )
    edges, own = pl.pallas_call(
        functools.partial(pack_kernel, dims),
        name="pack",
        out_shape=(
            pltpu.VMEM((HALO, heads * width + columns), bf16),
            pltpu.VMEM((2 * rows, columns), bf16),
        ),
        in_specs=[HBM, HBM, HBM],
        out_specs=(VMEM,) * 2,
        scratch_shapes=[pltpu.SemaphoreType.DMA((4,))],
        compiler_params=params,
    )(queries, keys, values)
    edges = send(edges, [(at, at + 1) for at in range(count - 1)])
    first = send(own, [(at, at + 1) for at in range(count - 1)])

    def scratch(extra):
        return [
            pltpu.VMEM((kv, 2 * LANES, rows // BLOCK * width), bf16),
            pltpu.VMEM((2 * (rows + extra), q_taps * width), bf16),
            pltpu.VMEM((2 * (rows + extra), q_taps * width), bf16),
            pltpu.VMEM((rows + extra, rows), f32),
            pltpu.VMEM((rows + extra, rows), f32),
            pltpu.VMEM((rows + extra, columns), bf16),
        ]

    state = [
        pltpu.VMEM((heads, rows), f32),
        pltpu.VMEM((heads, rows), f32),
        pltpu.VMEM((heads, width, rows), f32),
    ]
    taps, coef = pl.pallas_call(
        functools.partial(taps_kernel, dims),
        name="taps",
        out_shape=(
            pltpu.VMEM((heads, q_taps * BLOCK, 2 * LANES), bf16),
            pltpu.VMEM((q_taps * 16, LANES), f32),
        ),
        in_specs=[HBM],
        out_specs=(VMEM, VMEM),
        scratch_shapes=[pltpu.VMEM((q_taps, heads, k_taps), f32), pltpu.SemaphoreType.DMA],
        compiler_params=params,
        cost_estimate=cost(10**9),
    )(taps_in)
    edges, taps = lax.optimization_barrier((edges, taps))
    qcat, top, total, acc, corner = pl.pallas_call(
        functools.partial(own_kernel, dims),
        name="own_shard",
        out_shape=(
            pltpu.VMEM((heads, rows, q_taps * width), bf16),
            *state,
            pltpu.VMEM((heads, 2 * HALO, LANES), f32),
        ),
        in_specs=[HBM] + [VMEM] * 4,
        out_specs=(VMEM,) * 5,
        scratch_shapes=[
            pltpu.VMEM((rows, heads * width), bf16),
            pltpu.VMEM((rows + HALO, width), f32),
            *scratch(0)[:3],
            pltpu.VMEM((heads, rows, rows), f32),
            pltpu.VMEM((rows, columns), bf16),
            pltpu.VMEM((q_taps + k_taps - 1, rows + HALO + 16, LANES), f32),
            pltpu.VMEM((rows + 2 * HALO, LANES), f32),
            pltpu.VMEM((rows + HALO, LANES), f32),
            pltpu.SemaphoreType.DMA,
        ],
        compiler_params=params,
        cost_estimate=cost(6 * 10**9),
    )(queries, own, edges, taps, coef)
    before, message = own, first
    for step in range(1, count - 1):
        source, top = lax.optimization_barrier((message, top))
        passed = send(source, [(at, at + 1) for at in range(step, count - 1)])
        top, total, acc = pl.pallas_call(
            functools.partial(step_kernel, dims, step),
            name="shard_step",
            out_shape=tuple(state),
            in_specs=[VMEM] * 8,
            out_specs=(VMEM,) * 3,
            scratch_shapes=scratch(HALO),
            input_output_aliases={3: 0, 4: 1, 5: 2},
            compiler_params=params,
            cost_estimate=cost(5 * 10**9),
        )(qcat, taps, corner, top, total, acc, before, message)
        before, message = message, passed
    return pl.pallas_call(
        functools.partial(last_kernel, dims, count - 1),
        name="last_step",
        out_shape=jax.ShapeDtypeStruct((rows, heads * width), bf16),
        in_specs=[VMEM] * 10 + [SMEM] * 2,
        out_specs=HBM,
        scratch_shapes=[
            *state,
            pltpu.VMEM((rows, heads * width), bf16),
            pltpu.SemaphoreType.DMA((kv,)),
            *scratch(HALO),
        ],
        compiler_params=params,
        cost_estimate=cost(5 * 10**9),
    )(
        qcat, taps, corner, top, total, acc, before, message, own,
        norm_gain.reshape(1, -1), head_mix, bounds,
    )


def solution(mesh):
    return jax.shard_map(
        attend,
        mesh=mesh,
        in_specs=(
            P(("groups", "ctx"), "heads"),
            P(("groups", "ctx"), "heads"),
            P(("groups", "ctx"), "heads"),
            P("heads", None, None),
            P("heads", None, None),
            P("heads"),
            P("groups"),
        ),
        out_specs=P(("groups", "ctx"), "heads"),
        check_vma=False,
    )
```

```python
import functools

import jax
import jax.numpy as jnp
from jax import lax
from jax.experimental import pallas as pl
from jax.experimental.pallas import tpu as pltpu
from jax.sharding import PartitionSpec as P

EPSILON = 1e-06
NEG_FILL = -1e30
LANES = 128
HALO = 16
BLOCK = 64
SLOT = 16
TAIL = 8
FOLD_TAPS = 2


def dot(a, b):
    return jnp.dot(a, b, preferred_element_type=jnp.float32)


def dot_nt(a, b):
    return lax.dot_general(a, b, (((1,), (1,)), ((), ())), preferred_element_type=jnp.float32)


def dot_tn(a, b, precision=None):
    return lax.dot_general(
        a, b, (((0,), (0,)), ((), ())), precision=precision, preferred_element_type=jnp.float32
    )


def split(value):
    high = value.astype(jnp.bfloat16)
    return high, (value - high.astype(jnp.float32)).astype(jnp.bfloat16)


def slot_lane(h):
    return 2 * SLOT * (h % 4) + SLOT * (h // 4)


def fill_group(rhs, vals, g, body, after, dims):
    rows, _, _, width, _, _ = dims
    cols = slice(g * width, (g + 1) * width)
    for blk in range(rows // BLOCK):
        at = slice(blk * width, (blk + 1) * width)
        first, last = blk * BLOCK, blk * BLOCK + LANES
        if last <= rows:
            piece = body[first:last, cols]
        elif after is None:
            piece = jnp.concatenate(
                [body[first:rows, cols], jnp.zeros((last - rows, width), jnp.bfloat16)], 0
            )
        else:
            piece = jnp.concatenate([body[first:rows, cols], after[: last - rows, cols]], 0)
        rhs[g, :LANES, at] = piece
        rhs[g, LANES:, at] = piece
    vals[: rows - HALO, cols] = body[rows + HALO : 2 * rows, cols]
    if after is None:
        vals[rows - HALO : rows, cols] = jnp.zeros((HALO, width), jnp.bfloat16)
    else:
        vals[rows - HALO : rows, cols] = after[rows : rows + HALO, cols]


def fold_keys(kp, taps, rhs, h, g, dims):
    rows, _, _, width, q_taps, _ = dims
    for first in range(0, q_taps, FOLD_TAPS):
        last = min(q_taps, first + FOLD_TAPS)
        out = dot(taps[h, first * BLOCK : last * BLOCK], rhs[g])
        for a in range(first, last):
            for blk in range(rows // BLOCK):
                at, row = blk * BLOCK, (a - first) * BLOCK
                high, low = split(out[row : row + BLOCK, blk * width : (blk + 1) * width])
                kp[at : at + BLOCK, a * width : (a + 1) * width] = high
                kp[rows + at : rows + at + BLOCK, a * width : (a + 1) * width] = low


def first_window(kv_ref, g, width):
    cols = slice(g * width, (g + 1) * width)
    zeros = jnp.zeros((HALO, width), jnp.bfloat16)
    rest = jnp.zeros((LANES - 3 * HALO, width), jnp.bfloat16)
    window = jnp.concatenate([zeros, kv_ref[: 2 * HALO, cols], rest], 0)
    return jnp.concatenate([window, window], 0)


def first_folded(taps_ref, window, h, q_taps):
    taps = jnp.concatenate(
        [taps_ref[h, a * BLOCK : a * BLOCK + HALO] for a in range(q_taps)], 0
    )
    folded = dot(taps, window)
    folded = jnp.concatenate([folded[a * HALO : (a + 1) * HALO] for a in range(q_taps)], 1)
    return jnp.concatenate(split(folded), 0)


def update(scores, values, at, h, m_in, l_in, acc_in, m_ref, l_ref, acc_ref):
    old = m_in[h : h + 1, :]
    top = jnp.maximum(old, jnp.max(scores, axis=0, keepdims=True))
    weights = jnp.exp(scores - top)
    decay = jnp.exp(old - top)
    m_ref[h : h + 1, :] = top
    l_ref[h : h + 1, :] = l_in[h : h + 1, :] * decay + jnp.sum(weights, axis=0, keepdims=True)
    acc_ref[h] = acc_in[h] * decay + dot_tn(values[:, at], weights.astype(jnp.bfloat16))


def pack_kernel(dims, q_hbm, k_hbm, v_hbm, own_ref, sems):
    rows, _, kv, width, _, _ = dims
    columns = kv * width
    moves = [(k_hbm, own_ref.at[:rows]), (v_hbm, own_ref.at[rows : 2 * rows])]
    for i in range(q_hbm.shape[1] // columns):
        at = 2 * rows + i * TAIL
        source = q_hbm.at[rows - TAIL :, i * columns : (i + 1) * columns]
        moves.append((source, own_ref.at[at : at + TAIL]))
    copies = [pltpu.make_async_copy(*move, sems.at[i]) for i, move in enumerate(moves)]
    for copy in copies:
        copy.start()
    for copy in copies:
        copy.wait()


def taps_kernel(dims, conv_hbm, taps_ref, coef_ref, conv, sem):
    _, heads, _, width, q_taps, k_taps = dims
    k_edge = k_taps // 2
    copy = pltpu.make_async_copy(conv_hbm, conv, sem)
    copy.start()
    copy.wait()
    lane = lax.broadcasted_iota(jnp.int32, (heads, LANES), 1)
    owner = lane // (2 * SLOT) + 4 * ((lane // SLOT) % 2)
    spread = jnp.where(
        owner == lax.broadcasted_iota(jnp.int32, (heads, LANES), 0), 1.0, 0.0
    ).astype(jnp.float32)
    offset = lax.broadcasted_iota(jnp.int32, (k_taps, LANES), 1) % SLOT
    tap = lax.broadcasted_iota(jnp.int32, (k_taps, LANES), 0)
    for a in range(q_taps):
        weights = conv[a] * width ** (-0.5)
        base = jnp.zeros((heads, LANES), jnp.float32)
        for t in range(k_taps):
            base = jnp.where(lane == HALO + k_edge - t, weights[:, t : t + 1], base)
        for h in range(heads):
            tile = pltpu.roll(
                jnp.broadcast_to(base[h : h + 1], (BLOCK, LANES)), 0, 1, stride=1, stride_axis=0
            )
            high, low = split(tile)
            taps_ref[h, a * BLOCK : (a + 1) * BLOCK, :LANES] = high
            taps_ref[h, a * BLOCK : (a + 1) * BLOCK, LANES:] = low
        lanes = dot_tn(weights, spread, lax.Precision.HIGHEST)
        source = offset + tap - k_edge - a
        inside = (source >= 0) & (source < SLOT) & (offset < q_taps - 1 + k_edge)
        coef_ref[a * 16 : a * 16 + k_taps] = jnp.where(inside, lanes, 0.0)


def pack_head(packs, ring, h):
    lane = lax.broadcasted_iota(jnp.int32, ring.shape, 1)
    moved = []
    for first in range(0, ring.shape[0], 8):
        shift = (slot_lane(h) + HALO - first) % LANES
        piece = ring[first : first + 8]
        moved.append(pltpu.roll(piece, shift, 1) if shift else piece)
    mine = (lane - slot_lane(h)) % LANES < 2 * SLOT
    packs[h // 4] = jnp.where(mine, jnp.concatenate(moved, 0), packs[h // 4])


def skew(packs, heads):
    sub = lax.broadcasted_iota(jnp.int32, packs[0].shape, 0)
    for i in range(2 if heads > 4 else 1):
        for bit in (1, 2, 4):
            packs[i] = jnp.where(
                (sub & bit) != 0, pltpu.roll(packs[i], LANES - bit, 1), packs[i]
            )


def roll_band(rolled, packed_ref, order, delta):
    tall = packed_ref.shape[0]
    rolled[order, :8] = jnp.zeros((8, LANES), jnp.float32)
    shift = (-delta) % LANES
    value = packed_ref[...]
    rolled[order, 8 : 8 + tall] = pltpu.roll(value, shift, 1) if shift else value
    rolled[order, 8 + tall :] = jnp.zeros((8, LANES), jnp.float32)


def convolve_band(zband, rolled, coef, deltas, q_taps, k_taps, first):
    k_edge = k_taps // 2
    total = jnp.zeros((HALO, LANES), jnp.float32)
    for order, delta in deltas:
        for a in range(q_taps):
            t = k_edge + a + delta
            if 0 <= t < k_taps:
                at = 8 + first + k_edge - t
                row = a * 16 + t
                total = total + coef[row : row + 1, :] * rolled[order, at : at + HALO]
    zband[first : first + HALO] = total


def edge_kernel(dims, below, own, coef, qcat_in, qcat_ref, corner_ref, rolled, packed_ref, zband):
    rows, heads, kv, width, q_taps, k_taps = dims
    per = heads // kv
    k_edge = k_taps // 2
    tall = packed_ref.shape[0]
    lane = lax.broadcasted_iota(jnp.int32, (tall, LANES), 1)
    packs = [jnp.zeros((tall, LANES), jnp.float32) for _ in range(2)]
    for h in range(heads):
        g = h // per
        cols = slice(g * width, (g + 1) * width)
        at = 2 * rows + h // kv * TAIL
        tail = below[at : at + TAIL, h % kv * width : (h % kv + 1) * width].astype(jnp.float32)
        joined = jnp.concatenate([tail, qcat_in[h, :HALO, :width].astype(jnp.float32)], 0)
        for a in range(1, q_taps):
            shifted = joined[TAIL - a : TAIL - a + HALO].astype(jnp.bfloat16)
            qcat_ref[h, :HALO, a * width : (a + 1) * width] = shifted
        zeros = jnp.zeros((HALO - TAIL, width), jnp.float32)
        tail = jnp.concatenate([zeros, tail], 0).astype(jnp.bfloat16)
        near = jnp.concatenate([qcat_in[h, : LANES - HALO, :width], tail], 0)
        keys = jnp.concatenate([below[rows - HALO : rows, cols], own[: tall - HALO, cols]], 0)
        pack_head(packs, dot_nt(keys, near), h)
    skew(packs, heads)
    packed_ref[...] = jnp.where((lane // SLOT) % 2 == 0, packs[0], packs[1])
    deltas = list(enumerate(range(-k_edge - q_taps + 1, k_edge + 1)))
    for pair in deltas:
        roll_band(rolled, packed_ref, *pair)
    for first in (0, HALO):
        convolve_band(zband, rolled, coef, deltas, q_taps, k_taps, first)
    for h in range(heads):
        shift = (LANES - HALO - slot_lane(h)) % LANES
        corner_ref[h] = pltpu.roll(zband[...], shift, 1, stride=1, stride_axis=0)


def own_kernel(
    dims,
    q_hbm, kv_ref, taps_ref, coef,
    qcat_ref, m_ref, l_ref, acc_ref,
    q_ref, qf, rhs, kp0, kp1, sc, vals, rolled, zband, packed_ref, sem,
):
    rows, heads, kv, width, q_taps, k_taps = dims
    per = heads // kv
    k_edge = k_taps // 2
    reach = q_taps - 1 + k_edge
    copy = pltpu.make_async_copy(q_hbm, q_ref, sem)
    copy.start()
    for g in range(kv):
        fill_group(rhs, vals, g, kv_ref, None, dims)
    copy.wait()
    blocks = rows // LANES
    tall = rows + HALO
    lane = lax.broadcasted_iota(jnp.int32, (tall, LANES), 1)
    lane_small = lax.broadcasted_iota(jnp.int32, (HALO, LANES), 1)
    packs = [jnp.zeros((tall, LANES), jnp.float32) for _ in range(2)]
    for h in range(heads):
        g = h // per
        cols = slice(h * width, (h + 1) * width)
        kcols = slice(g * width, (g + 1) * width)
        qf[:HALO] = jnp.zeros((HALO, width), jnp.float32)
        qf[HALO:] = q_ref[:, cols].astype(jnp.float32)
        qcat_ref[h, :, :width] = q_ref[:, cols]
        for a in range(1, q_taps):
            qcat_ref[h, :, a * width : (a + 1) * width] = qf[
                HALO - a : HALO - a + rows
            ].astype(jnp.bfloat16)
        pieces = [jnp.zeros((HALO, LANES), jnp.float32)]
        for blk in range(blocks):
            key_blk = kv_ref[blk * LANES : (blk + 1) * LANES, kcols]
            last = min(rows, (blk + 2) * LANES)
            raw = dot_nt(key_blk, q_ref[blk * LANES : last, cols])
            if last == (blk + 2) * LANES:
                pieces.append(raw[: LANES - HALO, :LANES])
                pieces.append(
                    jnp.where(
                        lane_small < LANES // 2,
                        raw[LANES - HALO :, LANES:],
                        raw[LANES - HALO :, :LANES],
                    )
                )
            else:
                pieces.append(raw)
        ring = jnp.concatenate(pieces, 0)
        pack_head(packs, ring, h)
    skew(packs, heads)
    packed_ref[...] = jnp.where((lane // SLOT) % 2 == 0, packs[0], packs[1])
    deltas = list(enumerate(range(-k_edge - q_taps + 1, k_edge + 1)))
    roll_unit = functools.partial(roll_band, rolled, packed_ref)
    band_unit = functools.partial(convolve_band, zband, rolled, coef, deltas, q_taps, k_taps)
    units = [functools.partial(roll_unit, *pair) for pair in deltas]
    units += [functools.partial(band_unit, first) for first in range(0, tall, HALO)]
    zband[tall:] = jnp.zeros((HALO, LANES), jnp.float32)
    key_id = HALO + lax.broadcasted_iota(jnp.int32, (rows, rows), 0)
    row_id = lax.broadcasted_iota(jnp.int32, (rows, rows), 1)

    def finish_head(h):
        g = h // per
        base = slot_lane(h)
        strips = []
        for blk in range(blocks):
            at = 2 * HALO + blk * LANES
            tile = pltpu.roll(
                zband[at : at + LANES], (HALO - base) % LANES, 1, stride=1, stride_axis=0
            )
            strips.append(jnp.concatenate([tile] * blocks, 1))
        exact = jnp.concatenate(strips, 0)
        scores = jnp.where(row_id - key_id < reach, exact, sc[h])
        scores = jnp.where(key_id <= row_id, scores, NEG_FILL)
        top = jnp.max(scores, axis=0, keepdims=True)
        weights = jnp.where(key_id <= row_id, jnp.exp(scores - top), 0.0)
        m_ref[h : h + 1, :] = top
        l_ref[h : h + 1, :] = jnp.sum(weights, axis=0, keepdims=True)
        acc_ref[h] = dot_tn(vals[:, g * width : (g + 1) * width], weights.astype(jnp.bfloat16))

    kps = (kp0, kp1)
    early = max(1, heads - 3)
    share = -(-len(units) // early)
    done = 0
    for h in range(heads):
        fold_keys(kps[h % 2], taps_ref, rhs, h, h // per, dims)
        if h < early:
            for unit in units[h * share : (h + 1) * share]:
                unit()
        else:
            for _ in range(2):
                if done < h:
                    finish_head(done)
                    done += 1
        both = dot_nt(kps[h % 2][...], qcat_ref[h])
        sc[h] = both[:rows] + both[rows:]
    for h in range(done, heads):
        finish_head(h)


def first_positions(dims, qcat_ref, taps_ref, kv_ref, corner_ref, state_in, state):
    rows, heads, kv, width, q_taps, k_taps = dims
    per = heads // kv
    reach = q_taps - 1 + k_taps // 2
    key_id = lax.broadcasted_iota(jnp.int32, (HALO, rows), 0)
    row_id = lax.broadcasted_iota(jnp.int32, (HALO, rows), 1)
    for h in range(heads):
        g = h // per
        both = dot_nt(first_folded(taps_ref, first_window(kv_ref, g, width), h, q_taps), qcat_ref[h])
        scores = both[:HALO] + both[HALO:]
        exact = jnp.concatenate([corner_ref[h, HALO:]] * (rows // LANES), 1)
        scores = jnp.where(row_id - key_id < reach, exact, scores)
        scores = jnp.where(key_id <= row_id, scores, NEG_FILL)
        at = slice(g * width, (g + 1) * width)
        update(scores, kv_ref.at[rows : rows + HALO], at, h, *state_in, *state)


def add_shard(
    dims, step, extra, qcat_ref, taps_ref, corner_ref, body, after, state_in, state, scratch, finish
):
    rows, heads, kv, width, q_taps, k_taps = dims
    per = heads // kv
    reach = q_taps - 1 + k_taps // 2
    rhs, kp0, kp1, sc0, sc1, vals = scratch
    kps, scs = (kp0, kp1), (sc0, sc1)
    total = rows + HALO if extra else rows
    for g in range(kv):
        fill_group(rhs, vals, g, body, after, dims)
    if extra:
        vals[rows:] = body[rows : rows + HALO]
    key_id = lax.broadcasted_iota(jnp.int32, (2 * HALO, LANES), 0) - HALO
    row_id = lax.broadcasted_iota(jnp.int32, (2 * HALO, LANES), 1)

    def fold(h):
        fold_keys(kps[h % 2], taps_ref, rhs, h, h // per, dims)
        if extra:
            window = first_window(body, h // per, width)
            kps[h % 2][2 * rows :] = first_folded(taps_ref, window, h, q_taps)

    fold(0)
    for h in range(heads):
        g = h // per
        sc = scs[h % 2]
        both = dot_nt(kps[h % 2][: 2 * total], qcat_ref[h])
        sc[:rows] = both[:rows] + both[rows : 2 * rows]
        if extra:
            sc[rows:] = both[2 * rows : 2 * rows + HALO] + both[2 * rows + HALO :]
        if h + 1 < heads:
            fold(h + 1)
        if step == 1:
            at = slice(rows - 2 * HALO, rows)
            patch = sc[at, :LANES]
            patch = jnp.where(row_id - key_id < reach, corner_ref[h], patch)
            sc[at, :LANES] = jnp.where(key_id <= row_id, patch, NEG_FILL)
        at = slice(g * width, (g + 1) * width)
        update(sc[:total], vals.at[:total], at, h, *state_in, *state)
        if finish is not None and h % per == per - 1:
            finish(g)


def step_kernel(
    dims, step, qcat_ref, taps_ref, corner_ref, m_in, l_in, acc_in, after, body,
    m_ref, l_ref, acc_ref, *scratch
):
    place = lax.axis_index("ctx")
    states = (m_in, l_in, acc_in), (m_ref, l_ref, acc_ref)
    fixed = (qcat_ref, taps_ref, corner_ref, body, after, *states, scratch, None)

    @pl.when(place == step)
    def _():
        add_shard(dims, step, True, *fixed)

    @pl.when(place > step)
    def _():
        add_shard(dims, step, False, *fixed)


def last_kernel(
    dims, step, qcat_ref, taps_ref, corner_ref, m_in, l_in, acc_in, after, body, own,
    gain_ref, mix_ref, bounds_ref, o_hbm, m_ref, l_ref, acc_ref, out, sems, *scratch
):
    rows, heads, kv, width, _, _ = dims
    per = heads // kv
    place = lax.axis_index("ctx")
    row_pos = place * rows + lax.broadcasted_iota(jnp.int32, (rows, 1), 0)
    live = (row_pos >= bounds_ref[0]) & (row_pos < bounds_ref[1])
    states = (m_in, l_in, acc_in), (m_ref, l_ref, acc_ref)

    def copy_out(g):
        cols = pl.ds(g * per * width, per * width)
        return pltpu.make_async_copy(out.at[:, cols], o_hbm.at[:, cols], sems.at[g])

    def finish(g):
        probs = [acc_ref[h] * (1.0 / l_ref[h : h + 1, :]) for h in range(g * per, (g + 1) * per)]
        for a in range(per):
            blended = mix_ref[g, a, 0] * probs[0]
            for b in range(1, per):
                blended = blended + mix_ref[g, a, b] * probs[b]
            mean_sq = jnp.mean(blended * blended, axis=0, keepdims=True)
            normed = (blended * lax.rsqrt(mean_sq + EPSILON)).T
            at = slice((g * per + a) * width, (g * per + a + 1) * width)
            normed = jnp.where(live, normed * gain_ref[:, at], 0.0)
            out[:, at] = normed.astype(jnp.bfloat16)
        copy_out(g).start()

    @pl.when(place == step)
    def _():
        add_shard(
            dims, step, True, qcat_ref, taps_ref, corner_ref, body, after, *states, scratch, finish
        )

    @pl.when(place < step)
    def _():
        @pl.when(place == 0)
        def _():
            first_positions(dims, qcat_ref, taps_ref, own, corner_ref, *states)

        @pl.when(place > 0)
        def _():
            l_ref[...] = l_in[...]
            acc_ref[...] = acc_in[...]

        for g in range(kv):
            finish(g)

    for g in range(kv):
        copy_out(g).wait()


VMEM = pl.BlockSpec(memory_space=pltpu.VMEM)
SMEM = pl.BlockSpec(memory_space=pltpu.SMEM)
HBM = pl.BlockSpec(memory_space=pltpu.HBM)


def send(value, pairs):
    return lax.ppermute(value, "ctx", pairs)


def cost(flops):
    return pl.CostEstimate(flops=flops, bytes_accessed=2**20, transcendentals=0)


def attend(queries, keys, values, conv_kernel, head_mix, norm_gain, bounds):
    rows = queries.shape[0]
    kv, _ = head_mix.shape[:2]
    width = keys.shape[1] // kv
    heads, q_taps, k_taps = conv_kernel.shape
    count = lax.axis_size("ctx")
    dims = (rows, heads, kv, width, q_taps, k_taps)
    f32, bf16 = jnp.float32, jnp.bfloat16
    params = pltpu.CompilerParams(vmem_limit_bytes=28 * 2**20)

    columns = kv * width
    taps_in = conv_kernel.transpose(1, 0, 2)
    queries, keys, values, taps_in = (
        pltpu.with_memory_space_constraint(value, pltpu.HBM)
        for value in (queries, keys, values, taps_in)
    )
    stacked = heads // kv
    own = pl.pallas_call(
        functools.partial(pack_kernel, dims),
        name="pack",
        out_shape=pltpu.VMEM((2 * rows + stacked * TAIL, columns), bf16),
        in_specs=[HBM, HBM, HBM],
        out_specs=VMEM,
        scratch_shapes=[pltpu.SemaphoreType.DMA((2 + stacked,))],
        compiler_params=params,
    )(queries, keys, values)
    first = send(own, [(at, at + 1) for at in range(count - 1)])

    def scratch(extra):
        return [
            pltpu.VMEM((kv, 2 * LANES, rows // BLOCK * width), bf16),
            pltpu.VMEM((2 * (rows + extra), q_taps * width), bf16),
            pltpu.VMEM((2 * (rows + extra), q_taps * width), bf16),
            pltpu.VMEM((rows + extra, rows), f32),
            pltpu.VMEM((rows + extra, rows), f32),
            pltpu.VMEM((rows + extra, columns), bf16),
        ]

    state = [
        pltpu.VMEM((heads, rows), f32),
        pltpu.VMEM((heads, rows), f32),
        pltpu.VMEM((heads, width, rows), f32),
    ]
    taps, coef = pl.pallas_call(
        functools.partial(taps_kernel, dims),
        name="taps",
        out_shape=(
            pltpu.VMEM((heads, q_taps * BLOCK, 2 * LANES), bf16),
            pltpu.VMEM((q_taps * 16, LANES), f32),
        ),
        in_specs=[HBM],
        out_specs=(VMEM, VMEM),
        scratch_shapes=[pltpu.VMEM((q_taps, heads, k_taps), f32), pltpu.SemaphoreType.DMA],
        compiler_params=params,
        cost_estimate=cost(10**9),
    )(taps_in)
    qcat, top, total, acc = pl.pallas_call(
        functools.partial(own_kernel, dims),
        name="own_shard",
        out_shape=(
            pltpu.VMEM((heads, rows, q_taps * width), bf16),
            *state,
        ),
        in_specs=[HBM] + [VMEM] * 3,
        out_specs=(VMEM,) * 4,
        scratch_shapes=[
            pltpu.VMEM((rows, heads * width), bf16),
            pltpu.VMEM((rows + HALO, width), f32),
            *scratch(0)[:3],
            pltpu.VMEM((heads, rows, rows), f32),
            pltpu.VMEM((rows, columns), bf16),
            pltpu.VMEM((q_taps + k_taps - 1, rows + HALO + 16, LANES), f32),
            pltpu.VMEM((rows + 2 * HALO, LANES), f32),
            pltpu.VMEM((rows + HALO, LANES), f32),
            pltpu.SemaphoreType.DMA,
        ],
        compiler_params=params,
        cost_estimate=cost(6 * 10**9),
    )(queries, own, taps, coef)
    before, message, passed = own, first, None
    corner = None
    for step in range(1, count):
        if step + 1 < count:
            source, top = lax.optimization_barrier((message, top))
            passed = send(source, [(at, at + 1) for at in range(step, count - 1)])
        if step == 1:
            qcat, corner = pl.pallas_call(
                functools.partial(edge_kernel, dims),
                name="edge",
                out_shape=(
                    pltpu.VMEM((heads, rows, q_taps * width), bf16),
                    pltpu.VMEM((heads, 2 * HALO, LANES), f32),
                ),
                in_specs=[VMEM] * 4,
                out_specs=(VMEM,) * 2,
                scratch_shapes=[
                    pltpu.VMEM((q_taps + k_taps - 1, 3 * HALO + 16, LANES), f32),
                    pltpu.VMEM((3 * HALO, LANES), f32),
                    pltpu.VMEM((2 * HALO, LANES), f32),
                ],
                input_output_aliases={3: 0},
                compiler_params=params,
                cost_estimate=cost(10**9),
            )(message, own, coef, qcat)
        if step + 1 == count:
            break
        top, total, acc = pl.pallas_call(
            functools.partial(step_kernel, dims, step),
            name="shard_step",
            out_shape=tuple(state),
            in_specs=[VMEM] * 8,
            out_specs=(VMEM,) * 3,
            scratch_shapes=scratch(HALO),
            input_output_aliases={3: 0, 4: 1, 5: 2},
            compiler_params=params,
            cost_estimate=cost(5 * 10**9),
        )(qcat, taps, corner, top, total, acc, before, message)
        before, message = message, passed
    return pl.pallas_call(
        functools.partial(last_kernel, dims, count - 1),
        name="last_step",
        out_shape=jax.ShapeDtypeStruct((rows, heads * width), bf16),
        in_specs=[VMEM] * 10 + [SMEM] * 2,
        out_specs=HBM,
        scratch_shapes=[
            *state,
            pltpu.VMEM((rows, heads * width), bf16),
            pltpu.SemaphoreType.DMA((kv,)),
            *scratch(HALO),
        ],
        compiler_params=params,
        cost_estimate=cost(5 * 10**9),
    )(
        qcat, taps, corner, top, total, acc, before, message, own,
        norm_gain.reshape(1, -1), head_mix, bounds,
    )


def solution(mesh):
    return jax.shard_map(
        attend,
        mesh=mesh,
        in_specs=(
            P(("groups", "ctx"), "heads"),
            P(("groups", "ctx"), "heads"),
            P(("groups", "ctx"), "heads"),
            P("heads", None, None),
            P("heads", None, None),
            P("heads"),
            P("groups"),
        ),
        out_specs=P(("groups", "ctx"), "heads"),
        check_vma=False,
    )
```

```python
import functools

import jax
import jax.numpy as jnp
from jax import lax
from jax.experimental import pallas as pl
from jax.experimental.pallas import tpu as pltpu
from jax.sharding import PartitionSpec as P

EPSILON = 1e-06
NEG_FILL = -1e30
LANES = 128
HALO = 16
BLOCK = 64
SLOT = 16
TAIL = 8
FOLD_TAPS = 2


def dot(a, b):
    return jnp.dot(a, b, preferred_element_type=jnp.float32)


def dot_nt(a, b):
    return lax.dot_general(a, b, (((1,), (1,)), ((), ())), preferred_element_type=jnp.float32)


def dot_tn(a, b, precision=None):
    return lax.dot_general(
        a, b, (((0,), (0,)), ((), ())), precision=precision, preferred_element_type=jnp.float32
    )


def split(value):
    high = value.astype(jnp.bfloat16)
    return high, (value - high.astype(jnp.float32)).astype(jnp.bfloat16)


def slot_lane(h):
    return 2 * SLOT * (h % 4) + SLOT * (h // 4)


def fill_group(rhs, vals, g, body, after, dims):
    rows, _, _, width, _, _ = dims
    cols = slice(g * width, (g + 1) * width)
    for blk in range(rows // BLOCK):
        at = slice(blk * width, (blk + 1) * width)
        first, last = blk * BLOCK, blk * BLOCK + LANES
        if last <= rows:
            piece = body[first:last, cols]
        elif after is None:
            piece = jnp.concatenate(
                [body[first:rows, cols], jnp.zeros((last - rows, width), jnp.bfloat16)], 0
            )
        else:
            piece = jnp.concatenate([body[first:rows, cols], after[: last - rows, cols]], 0)
        rhs[g, :LANES, at] = piece
        rhs[g, LANES:, at] = piece
    vals[: rows - HALO, cols] = body[rows + HALO : 2 * rows, cols]
    if after is None:
        vals[rows - HALO : rows, cols] = jnp.zeros((HALO, width), jnp.bfloat16)
    else:
        vals[rows - HALO : rows, cols] = after[rows : rows + HALO, cols]


def fold_keys(kp, taps, rhs, h, g, dims):
    rows, _, _, width, q_taps, _ = dims
    for first in range(0, q_taps, FOLD_TAPS):
        last = min(q_taps, first + FOLD_TAPS)
        out = dot(taps[h, first * BLOCK : last * BLOCK], rhs[g])
        for a in range(first, last):
            for blk in range(rows // BLOCK):
                at, row = blk * BLOCK, (a - first) * BLOCK
                high, low = split(out[row : row + BLOCK, blk * width : (blk + 1) * width])
                kp[at : at + BLOCK, a * width : (a + 1) * width] = high
                kp[rows + at : rows + at + BLOCK, a * width : (a + 1) * width] = low


def first_window(kv_ref, g, width):
    cols = slice(g * width, (g + 1) * width)
    zeros = jnp.zeros((HALO, width), jnp.bfloat16)
    rest = jnp.zeros((LANES - 3 * HALO, width), jnp.bfloat16)
    window = jnp.concatenate([zeros, kv_ref[: 2 * HALO, cols], rest], 0)
    return jnp.concatenate([window, window], 0)


def first_folded(taps_ref, window, h, q_taps):
    taps = jnp.concatenate(
        [taps_ref[h, a * BLOCK : a * BLOCK + HALO] for a in range(q_taps)], 0
    )
    folded = dot(taps, window)
    folded = jnp.concatenate([folded[a * HALO : (a + 1) * HALO] for a in range(q_taps)], 1)
    return jnp.concatenate(split(folded), 0)


def update(scores, values, at, h, m_in, l_in, acc_in, m_ref, l_ref, acc_ref):
    old = m_in[h : h + 1, :]
    top = jnp.maximum(old, jnp.max(scores, axis=0, keepdims=True))
    weights = jnp.exp(scores - top)
    decay = jnp.exp(old - top)
    m_ref[h : h + 1, :] = top
    l_ref[h : h + 1, :] = l_in[h : h + 1, :] * decay + jnp.sum(weights, axis=0, keepdims=True)
    acc_ref[h] = acc_in[h] * decay + dot_tn(values[:, at], weights.astype(jnp.bfloat16))


def pack_kernel(dims, q_hbm, k_hbm, v_hbm, conv_hbm, own_ref, conv_ref, sems):
    rows, _, kv, width, _, _ = dims
    columns = kv * width
    moves = [(k_hbm, own_ref.at[:rows]), (v_hbm, own_ref.at[rows : 2 * rows]), (conv_hbm, conv_ref)]
    for i in range(q_hbm.shape[1] // columns):
        at = 2 * rows + i * TAIL
        source = q_hbm.at[rows - TAIL :, i * columns : (i + 1) * columns]
        moves.append((source, own_ref.at[at : at + TAIL]))
    copies = [pltpu.make_async_copy(*move, sems.at[i]) for i, move in enumerate(moves)]
    for copy in copies:
        copy.start()
    for copy in copies:
        copy.wait()


def taps_kernel(dims, conv, q_hbm, taps_ref, coef_ref, q_ref, sem):
    _, heads, _, width, q_taps, k_taps = dims
    k_edge = k_taps // 2
    copy = pltpu.make_async_copy(q_hbm, q_ref, sem)
    copy.start()
    lane = lax.broadcasted_iota(jnp.int32, (heads, LANES), 1)
    owner = lane // (2 * SLOT) + 4 * ((lane // SLOT) % 2)
    spread = jnp.where(
        owner == lax.broadcasted_iota(jnp.int32, (heads, LANES), 0), 1.0, 0.0
    ).astype(jnp.float32)
    offset = lax.broadcasted_iota(jnp.int32, (k_taps, LANES), 1) % SLOT
    tap = lax.broadcasted_iota(jnp.int32, (k_taps, LANES), 0)
    for a in range(q_taps):
        weights = conv[a] * width ** (-0.5)
        base = jnp.zeros((heads, LANES), jnp.float32)
        for t in range(k_taps):
            base = jnp.where(lane == HALO + k_edge - t, weights[:, t : t + 1], base)
        for h in range(heads):
            tile = pltpu.roll(
                jnp.broadcast_to(base[h : h + 1], (BLOCK, LANES)), 0, 1, stride=1, stride_axis=0
            )
            high, low = split(tile)
            taps_ref[h, a * BLOCK : (a + 1) * BLOCK, :LANES] = high
            taps_ref[h, a * BLOCK : (a + 1) * BLOCK, LANES:] = low
        lanes = dot_tn(weights, spread, lax.Precision.HIGHEST)
        source = offset + tap - k_edge - a
        inside = (source >= 0) & (source < SLOT) & (offset < q_taps - 1 + k_edge)
        coef_ref[a * 16 : a * 16 + k_taps] = jnp.where(inside, lanes, 0.0)
    copy.wait()


def pack_head(packs, ring, h):
    lane = lax.broadcasted_iota(jnp.int32, ring.shape, 1)
    moved = []
    for first in range(0, ring.shape[0], 8):
        shift = (slot_lane(h) + HALO - first) % LANES
        piece = ring[first : first + 8]
        moved.append(pltpu.roll(piece, shift, 1) if shift else piece)
    mine = (lane - slot_lane(h)) % LANES < 2 * SLOT
    packs[h // 4] = jnp.where(mine, jnp.concatenate(moved, 0), packs[h // 4])


def skew(packs, heads):
    sub = lax.broadcasted_iota(jnp.int32, packs[0].shape, 0)
    for i in range(2 if heads > 4 else 1):
        for bit in (1, 2, 4):
            packs[i] = jnp.where(
                (sub & bit) != 0, pltpu.roll(packs[i], LANES - bit, 1), packs[i]
            )


def roll_band(rolled, packed_ref, order, delta):
    tall = packed_ref.shape[0]
    rolled[order, :8] = jnp.zeros((8, LANES), jnp.float32)
    shift = (-delta) % LANES
    value = packed_ref[...]
    rolled[order, 8 : 8 + tall] = pltpu.roll(value, shift, 1) if shift else value
    rolled[order, 8 + tall :] = jnp.zeros((8, LANES), jnp.float32)


def convolve_band(zband, rolled, coef, deltas, q_taps, k_taps, first):
    k_edge = k_taps // 2
    total = jnp.zeros((HALO, LANES), jnp.float32)
    for order, delta in deltas:
        for a in range(q_taps):
            t = k_edge + a + delta
            if 0 <= t < k_taps:
                at = 8 + first + k_edge - t
                row = a * 16 + t
                total = total + coef[row : row + 1, :] * rolled[order, at : at + HALO]
    zband[first : first + HALO] = total


def edge_kernel(dims, below, own, coef, qcat_in, qcat_ref, corner_ref, rolled, packed_ref, zband):
    rows, heads, kv, width, q_taps, k_taps = dims
    per = heads // kv
    k_edge = k_taps // 2
    tall = packed_ref.shape[0]
    lane = lax.broadcasted_iota(jnp.int32, (tall, LANES), 1)
    packs = [jnp.zeros((tall, LANES), jnp.float32) for _ in range(2)]
    for h in range(heads):
        g = h // per
        cols = slice(g * width, (g + 1) * width)
        at = 2 * rows + h // kv * TAIL
        tail = below[at : at + TAIL, h % kv * width : (h % kv + 1) * width].astype(jnp.float32)
        joined = jnp.concatenate([tail, qcat_in[h, :HALO, :width].astype(jnp.float32)], 0)
        for a in range(1, q_taps):
            shifted = joined[TAIL - a : TAIL - a + HALO].astype(jnp.bfloat16)
            qcat_ref[h, :HALO, a * width : (a + 1) * width] = shifted
        zeros = jnp.zeros((HALO - TAIL, width), jnp.float32)
        tail = jnp.concatenate([zeros, tail], 0).astype(jnp.bfloat16)
        near = jnp.concatenate([qcat_in[h, : LANES - HALO, :width], tail], 0)
        keys = jnp.concatenate([below[rows - HALO : rows, cols], own[: tall - HALO, cols]], 0)
        pack_head(packs, dot_nt(keys, near), h)
    skew(packs, heads)
    packed_ref[...] = jnp.where((lane // SLOT) % 2 == 0, packs[0], packs[1])
    deltas = list(enumerate(range(-k_edge - q_taps + 1, k_edge + 1)))
    for pair in deltas:
        roll_band(rolled, packed_ref, *pair)
    for first in (0, HALO):
        convolve_band(zband, rolled, coef, deltas, q_taps, k_taps, first)
    for h in range(heads):
        shift = (LANES - HALO - slot_lane(h)) % LANES
        corner_ref[h] = pltpu.roll(zband[...], shift, 1, stride=1, stride_axis=0)


def own_kernel(
    dims,
    q_ref, kv_ref, taps_ref, coef,
    qcat_ref, m_ref, l_ref, acc_ref,
    qf, rhs, kp0, kp1, sc, vals, rolled, zband, packed_ref,
):
    rows, heads, kv, width, q_taps, k_taps = dims
    per = heads // kv
    k_edge = k_taps // 2
    reach = q_taps - 1 + k_edge
    for g in range(kv):
        fill_group(rhs, vals, g, kv_ref, None, dims)
    blocks = rows // LANES
    tall = rows + HALO
    lane = lax.broadcasted_iota(jnp.int32, (tall, LANES), 1)
    lane_small = lax.broadcasted_iota(jnp.int32, (HALO, LANES), 1)
    packs = [jnp.zeros((tall, LANES), jnp.float32) for _ in range(2)]
    for h in range(heads):
        g = h // per
        cols = slice(h * width, (h + 1) * width)
        kcols = slice(g * width, (g + 1) * width)
        qf[:HALO] = jnp.zeros((HALO, width), jnp.float32)
        qf[HALO:] = q_ref[:, cols].astype(jnp.float32)
        qcat_ref[h, :, :width] = q_ref[:, cols]
        for a in range(1, q_taps):
            qcat_ref[h, :, a * width : (a + 1) * width] = qf[
                HALO - a : HALO - a + rows
            ].astype(jnp.bfloat16)
        pieces = [jnp.zeros((HALO, LANES), jnp.float32)]
        for blk in range(blocks):
            key_blk = kv_ref[blk * LANES : (blk + 1) * LANES, kcols]
            last = min(rows, (blk + 2) * LANES)
            raw = dot_nt(key_blk, q_ref[blk * LANES : last, cols])
            if last == (blk + 2) * LANES:
                pieces.append(raw[: LANES - HALO, :LANES])
                pieces.append(
                    jnp.where(
                        lane_small < LANES // 2,
                        raw[LANES - HALO :, LANES:],
                        raw[LANES - HALO :, :LANES],
                    )
                )
            else:
                pieces.append(raw)
        ring = jnp.concatenate(pieces, 0)
        pack_head(packs, ring, h)
    skew(packs, heads)
    packed_ref[...] = jnp.where((lane // SLOT) % 2 == 0, packs[0], packs[1])
    deltas = list(enumerate(range(-k_edge - q_taps + 1, k_edge + 1)))
    roll_unit = functools.partial(roll_band, rolled, packed_ref)
    band_unit = functools.partial(convolve_band, zband, rolled, coef, deltas, q_taps, k_taps)
    units = [functools.partial(roll_unit, *pair) for pair in deltas]
    units += [functools.partial(band_unit, first) for first in range(0, tall, HALO)]
    zband[tall:] = jnp.zeros((HALO, LANES), jnp.float32)
    key_id = HALO + lax.broadcasted_iota(jnp.int32, (rows, rows), 0)
    row_id = lax.broadcasted_iota(jnp.int32, (rows, rows), 1)

    def finish_head(h):
        g = h // per
        base = slot_lane(h)
        strips = []
        for blk in range(blocks):
            at = 2 * HALO + blk * LANES
            tile = pltpu.roll(
                zband[at : at + LANES], (HALO - base) % LANES, 1, stride=1, stride_axis=0
            )
            strips.append(jnp.concatenate([tile] * blocks, 1))
        exact = jnp.concatenate(strips, 0)
        scores = jnp.where(row_id - key_id < reach, exact, sc[h])
        scores = jnp.where(key_id <= row_id, scores, NEG_FILL)
        top = jnp.max(scores, axis=0, keepdims=True)
        weights = jnp.where(key_id <= row_id, jnp.exp(scores - top), 0.0)
        m_ref[h : h + 1, :] = top
        l_ref[h : h + 1, :] = jnp.sum(weights, axis=0, keepdims=True)
        acc_ref[h] = dot_tn(vals[:, g * width : (g + 1) * width], weights.astype(jnp.bfloat16))

    kps = (kp0, kp1)
    early = max(1, heads - 3)
    share = -(-len(units) // early)
    done = 0
    for h in range(heads):
        fold_keys(kps[h % 2], taps_ref, rhs, h, h // per, dims)
        if h < early:
            for unit in units[h * share : (h + 1) * share]:
                unit()
        else:
            for _ in range(2):
                if done < h:
                    finish_head(done)
                    done += 1
        both = dot_nt(kps[h % 2][...], qcat_ref[h])
        sc[h] = both[:rows] + both[rows:]
    for h in range(done, heads):
        finish_head(h)


def first_positions(dims, qcat_ref, taps_ref, kv_ref, corner_ref, state_in, state):
    rows, heads, kv, width, q_taps, k_taps = dims
    per = heads // kv
    reach = q_taps - 1 + k_taps // 2
    key_id = lax.broadcasted_iota(jnp.int32, (HALO, rows), 0)
    row_id = lax.broadcasted_iota(jnp.int32, (HALO, rows), 1)
    for h in range(heads):
        g = h // per
        both = dot_nt(first_folded(taps_ref, first_window(kv_ref, g, width), h, q_taps), qcat_ref[h])
        scores = both[:HALO] + both[HALO:]
        exact = jnp.concatenate([corner_ref[h, HALO:]] * (rows // LANES), 1)
        scores = jnp.where(row_id - key_id < reach, exact, scores)
        scores = jnp.where(key_id <= row_id, scores, NEG_FILL)
        at = slice(g * width, (g + 1) * width)
        update(scores, kv_ref.at[rows : rows + HALO], at, h, *state_in, *state)


def add_shard(
    dims, step, extra, qcat_ref, taps_ref, corner_ref, body, after, state_in, state, scratch, finish
):
    rows, heads, kv, width, q_taps, k_taps = dims
    per = heads // kv
    reach = q_taps - 1 + k_taps // 2
    rhs, kp0, kp1, sc0, sc1, vals = scratch
    kps, scs = (kp0, kp1), (sc0, sc1)
    total = rows + HALO if extra else rows
    if extra:
        vals[rows:] = body[rows : rows + HALO]
    key_id = lax.broadcasted_iota(jnp.int32, (2 * HALO, LANES), 0) - HALO
    row_id = lax.broadcasted_iota(jnp.int32, (2 * HALO, LANES), 1)

    def fold(h):
        if h % per == 0:
            fill_group(rhs, vals, h // per, body, after, dims)
        fold_keys(kps[h % 2], taps_ref, rhs, h, h // per, dims)
        if extra:
            window = first_window(body, h // per, width)
            kps[h % 2][2 * rows :] = first_folded(taps_ref, window, h, q_taps)

    fold(0)
    for h in range(heads):
        g = h // per
        sc = scs[h % 2]
        both = dot_nt(kps[h % 2][: 2 * total], qcat_ref[h])
        sc[:rows] = both[:rows] + both[rows : 2 * rows]
        if extra:
            sc[rows:] = both[2 * rows : 2 * rows + HALO] + both[2 * rows + HALO :]
        if h + 1 < heads:
            fold(h + 1)
        if step == 1:
            at = slice(rows - 2 * HALO, rows)
            patch = sc[at, :LANES]
            patch = jnp.where(row_id - key_id < reach, corner_ref[h], patch)
            sc[at, :LANES] = jnp.where(key_id <= row_id, patch, NEG_FILL)
        at = slice(g * width, (g + 1) * width)
        update(sc[:total], vals.at[:total], at, h, *state_in, *state)
        if finish is not None and h % per == per - 1:
            finish(g)


def step_kernel(
    dims, step, qcat_ref, taps_ref, corner_ref, m_in, l_in, acc_in, after, body,
    m_ref, l_ref, acc_ref, *scratch
):
    place = lax.axis_index("ctx")
    states = (m_in, l_in, acc_in), (m_ref, l_ref, acc_ref)
    fixed = (qcat_ref, taps_ref, corner_ref, body, after, *states, scratch, None)

    @pl.when(place == step)
    def _():
        add_shard(dims, step, True, *fixed)

    @pl.when(place > step)
    def _():
        add_shard(dims, step, False, *fixed)


def last_kernel(
    dims, step, qcat_ref, taps_ref, corner_ref, m_in, l_in, acc_in, after, body, own,
    gain_ref, mix_ref, bounds_ref, o_hbm, m_ref, l_ref, acc_ref, out, sems, *scratch
):
    rows, heads, kv, width, _, _ = dims
    per = heads // kv
    place = lax.axis_index("ctx")
    row_pos = place * rows + lax.broadcasted_iota(jnp.int32, (rows, 1), 0)
    live = (row_pos >= bounds_ref[0]) & (row_pos < bounds_ref[1])
    states = (m_in, l_in, acc_in), (m_ref, l_ref, acc_ref)

    def copy_out(h):
        cols = pl.ds(h * width, width)
        return pltpu.make_async_copy(out.at[:, cols], o_hbm.at[:, cols], sems.at[h])

    def finish(g):
        probs = [acc_ref[h] * (1.0 / l_ref[h : h + 1, :]) for h in range(g * per, (g + 1) * per)]
        for a in range(per):
            blended = mix_ref[g, a, 0] * probs[0]
            for b in range(1, per):
                blended = blended + mix_ref[g, a, b] * probs[b]
            mean_sq = jnp.mean(blended * blended, axis=0, keepdims=True)
            normed = (blended * lax.rsqrt(mean_sq + EPSILON)).T
            at = slice((g * per + a) * width, (g * per + a + 1) * width)
            normed = jnp.where(live, normed * gain_ref[:, at], 0.0)
            out[:, at] = normed.astype(jnp.bfloat16)
            copy_out(g * per + a).start()

    @pl.when(place == step)
    def _():
        add_shard(
            dims, step, True, qcat_ref, taps_ref, corner_ref, body, after, *states, scratch, finish
        )

    @pl.when(place < step)
    def _():
        @pl.when(place == 0)
        def _():
            first_positions(dims, qcat_ref, taps_ref, own, corner_ref, *states)

        @pl.when(place > 0)
        def _():
            l_ref[...] = l_in[...]
            acc_ref[...] = acc_in[...]

        for g in range(kv):
            finish(g)

    for h in range(heads):
        copy_out(h).wait()


VMEM = pl.BlockSpec(memory_space=pltpu.VMEM)
SMEM = pl.BlockSpec(memory_space=pltpu.SMEM)
HBM = pl.BlockSpec(memory_space=pltpu.HBM)


def send(value, pairs):
    return lax.ppermute(value, "ctx", pairs)


def cost(flops):
    return pl.CostEstimate(flops=flops, bytes_accessed=2**20, transcendentals=0)


def attend(queries, keys, values, conv_kernel, head_mix, norm_gain, bounds):
    rows = queries.shape[0]
    kv, _ = head_mix.shape[:2]
    width = keys.shape[1] // kv
    heads, q_taps, k_taps = conv_kernel.shape
    count = lax.axis_size("ctx")
    dims = (rows, heads, kv, width, q_taps, k_taps)
    f32, bf16 = jnp.float32, jnp.bfloat16
    params = pltpu.CompilerParams(vmem_limit_bytes=28 * 2**20)

    columns = kv * width
    taps_in = conv_kernel.transpose(1, 0, 2)
    queries, keys, values, taps_in = (
        pltpu.with_memory_space_constraint(value, pltpu.HBM)
        for value in (queries, keys, values, taps_in)
    )
    stacked = heads // kv
    own, taps_in = pl.pallas_call(
        functools.partial(pack_kernel, dims),
        name="pack",
        out_shape=(
            pltpu.VMEM((2 * rows + stacked * TAIL, columns), bf16),
            pltpu.VMEM((q_taps, heads, k_taps), f32),
        ),
        in_specs=[HBM] * 4,
        out_specs=(VMEM, VMEM),
        scratch_shapes=[pltpu.SemaphoreType.DMA((3 + stacked,))],
        compiler_params=params,
    )(queries, keys, values, taps_in)
    first = send(own, [(at, at + 1) for at in range(count - 1)])

    def scratch(extra):
        return [
            pltpu.VMEM((kv, 2 * LANES, rows // BLOCK * width), bf16),
            pltpu.VMEM((2 * (rows + extra), q_taps * width), bf16),
            pltpu.VMEM((2 * (rows + extra), q_taps * width), bf16),
            pltpu.VMEM((rows + extra, rows), f32),
            pltpu.VMEM((rows + extra, rows), f32),
            pltpu.VMEM((rows + extra, columns), bf16),
        ]

    state = [
        pltpu.VMEM((heads, rows), f32),
        pltpu.VMEM((heads, rows), f32),
        pltpu.VMEM((heads, width, rows), f32),
    ]
    taps, coef, queries = pl.pallas_call(
        functools.partial(taps_kernel, dims),
        name="taps",
        out_shape=(
            pltpu.VMEM((heads, q_taps * BLOCK, 2 * LANES), bf16),
            pltpu.VMEM((q_taps * 16, LANES), f32),
            pltpu.VMEM((rows, heads * width), bf16),
        ),
        in_specs=[VMEM, HBM],
        out_specs=(VMEM,) * 3,
        scratch_shapes=[pltpu.SemaphoreType.DMA],
        compiler_params=params,
        cost_estimate=cost(10**9),
    )(taps_in, queries)
    qcat, top, total, acc = pl.pallas_call(
        functools.partial(own_kernel, dims),
        name="own_shard",
        out_shape=(
            pltpu.VMEM((heads, rows, q_taps * width), bf16),
            *state,
        ),
        in_specs=[VMEM] * 4,
        out_specs=(VMEM,) * 4,
        scratch_shapes=[
            pltpu.VMEM((rows + HALO, width), f32),
            *scratch(0)[:3],
            pltpu.VMEM((heads, rows, rows), f32),
            pltpu.VMEM((rows, columns), bf16),
            pltpu.VMEM((q_taps + k_taps - 1, rows + HALO + 16, LANES), f32),
            pltpu.VMEM((rows + 2 * HALO, LANES), f32),
            pltpu.VMEM((rows + HALO, LANES), f32),
        ],
        compiler_params=params,
        cost_estimate=cost(6 * 10**9),
    )(queries, own, taps, coef)
    before, message, passed = own, first, None
    corner = None
    for step in range(1, count):
        if step + 1 < count:
            source, top = lax.optimization_barrier((message, top))
            passed = send(source, [(at, at + 1) for at in range(step, count - 1)])
        if step == 1:
            qcat, corner = pl.pallas_call(
                functools.partial(edge_kernel, dims),
                name="edge",
                out_shape=(
                    pltpu.VMEM((heads, rows, q_taps * width), bf16),
                    pltpu.VMEM((heads, 2 * HALO, LANES), f32),
                ),
                in_specs=[VMEM] * 4,
                out_specs=(VMEM,) * 2,
                scratch_shapes=[
                    pltpu.VMEM((q_taps + k_taps - 1, 3 * HALO + 16, LANES), f32),
                    pltpu.VMEM((3 * HALO, LANES), f32),
                    pltpu.VMEM((2 * HALO, LANES), f32),
                ],
                input_output_aliases={3: 0},
                compiler_params=params,
                cost_estimate=cost(10**9),
            )(message, own, coef, qcat)
        if step + 1 == count:
            break
        top, total, acc = pl.pallas_call(
            functools.partial(step_kernel, dims, step),
            name="shard_step",
            out_shape=tuple(state),
            in_specs=[VMEM] * 8,
            out_specs=(VMEM,) * 3,
            scratch_shapes=scratch(HALO),
            input_output_aliases={3: 0, 4: 1, 5: 2},
            compiler_params=params,
            cost_estimate=cost(5 * 10**9),
        )(qcat, taps, corner, top, total, acc, before, message)
        before, message = message, passed
    return pl.pallas_call(
        functools.partial(last_kernel, dims, count - 1),
        name="last_step",
        out_shape=jax.ShapeDtypeStruct((rows, heads * width), bf16),
        in_specs=[VMEM] * 10 + [SMEM] * 2,
        out_specs=HBM,
        scratch_shapes=[
            *state,
            pltpu.VMEM((rows, heads * width), bf16),
            pltpu.SemaphoreType.DMA((heads,)),
            *scratch(HALO),
        ],
        compiler_params=params,
        cost_estimate=cost(5 * 10**9),
    )(
        qcat, taps, corner, top, total, acc, before, message, own,
        norm_gain.reshape(1, -1), head_mix, bounds,
    )


def solution(mesh):
    return jax.shard_map(
        attend,
        mesh=mesh,
        in_specs=(
            P(("groups", "ctx"), "heads"),
            P(("groups", "ctx"), "heads"),
            P(("groups", "ctx"), "heads"),
            P("heads", None, None),
            P("heads", None, None),
            P("heads"),
            P("groups"),
        ),
        out_specs=P(("groups", "ctx"), "heads"),
        check_vma=False,
    )
```
